32 devices in a mesh: groups: 2 (over y), slabx: 4 (over z), slaby: 2 (over x), section: 2 (over core).
Axes of the slice: x: 2, y: 2, z: 4, core: 2. Of those that a mesh axis runs over, the one named last changes fastest.
Arguments:
- nodes: bfloat16 [4, 6144, 512], P(None, ('groups', 'slabx', 'slaby')), parts along dimension 1, may hold values from -6 to 6
- tile_index: int32 [48, 4], P(('groups', 'slabx', 'slaby')), parts along dimension 0, may hold values from 0 to 6, as said below
- tile_values: bfloat16 [48, 4, 128, 128], P(('groups', 'slabx', 'slaby')), parts along dimension 0, may hold values from -0.25 to 0.25
- halo_rows: int32 [16, 4, 128], P(('groups', 'slabx', 'slaby')), parts along dimension 0, may hold values from 0 to 383, as said below
- w_msg: bfloat16 [2, 512, 512], P('section'), may hold values from -0.25 to 0.25
- w_in: bfloat16 [2, 1024, 512], P('section'), may hold values from -0.1875 to 0.1875
- w_out: bfloat16 [2, 512, 512], P('section'), may hold values from -0.25 to 0.25
- bias: float32 [2, 512], P('section'), may hold values from -3 to 3
- gain: float32 [2, 512], P('section'), may hold values from 0.1 to 1.9
Outputs:
- updated: bfloat16 [4, 6144, 512], P('section', ('groups', 'slabx', 'slaby')), parts along dimension 1
The draws below stay inside these ranges and needn't reach their ends.
There are 2 independent parts, one for each index of `groups`. The reference program is written for one: setup_inputs(seed, part) draws one part's arguments, and reference() takes and returns one part's arrays. A program takes and returns all parts, laid end to end along the dimension named above; an argument that names none is the same for every part. Nothing has to cross between parts.
Inputs may be any that keep to these rules, and one draw needn't show every extreme that they name: `tile_index`: row tile r of a slab lists itself first, then one tile of its own slab, then two of the halo tiles 3 .. 6; all four halo tiles appear in every slab's lists. `halo_rows`: each list holds 128 distinct local rows of its slab, among them row 0 and row 383.
All inputs are finite; a program needn't handle non-finite values.
Results may differ from the reference program's by a relative error of at most 0.013.
Values may be sent and summed in bfloat16 or wider, within the bound.
No kernel may reach another device: no remote copies, remote signals or barrier semaphores. Data moves between devices by JAX's collectives and lax.ppermute only.
A program may use at most 64 MiB of HBM per device.

```python
import jax
import jax.numpy as jnp
from jax import lax

D = 512
TILE = 128
K = 4
TL = 3
MB = 4
HALO = 128
LAYERS = 2
NODE_DEV = 384
SLABS = 8
NODES = 3072
TILES = 24
N_SLABX = 4
N_SLABY = 2


def draw_tile_index(key, part):
    slab_count = TILES // TL
    keys = jax.random.split(jax.random.fold_in(key, 11), slab_count)

    def one_slab(slab_key):
        first_key, second_key = jax.random.split(slab_key)
        rowpos = jnp.arange(TL, dtype=jnp.int32)
        other = jax.random.randint(first_key, (TL,), 0, TL, dtype=jnp.int32)
        order = jax.random.permutation(second_key, 4).astype(jnp.int32)
        first_halo = TL + order[2 * rowpos % 4]
        second_halo = TL + order[(2 * rowpos + 1) % 4]
        return jnp.stack([rowpos, other, first_halo, second_halo], axis=1).astype(jnp.int32)
    return jax.vmap(one_slab)(keys).reshape(TILES, K)


def draw_halo_rows(key, part):
    keys = jax.random.split(jax.random.fold_in(key, 23), SLABS * 4)

    def one_list(list_key):
        inner_key, order_key = jax.random.split(list_key)
        middle = jax.random.permutation(inner_key, NODE_DEV - 2)[:HALO - 2].astype(jnp.int32) + 1
        ends = jnp.array([0, NODE_DEV - 1], dtype=jnp.int32)
        rows = jnp.concatenate([ends, middle]).astype(jnp.int32)
        return rows[jax.random.permutation(order_key, HALO)].astype(jnp.int32)
    return jax.vmap(one_list)(keys).reshape(SLABS, 4, HALO)


def steps_of(key, shape, shards, smallest, largest):
    def one(axis_at, blocks):
        heights = jax.random.uniform(jax.random.fold_in(jax.random.fold_in(key, 6), axis_at), (blocks,), jnp.float32, smallest / len(shards), largest / len(shards))
        return jnp.repeat(jnp.exp(heights), shape[axis_at] // blocks).reshape((-1,) + (1,) * (len(shape) - axis_at - 1))

    loudness = one(*shards[0])
    for cut in shards[1:]:
        loudness = loudness * one(*cut)
    return loudness


def gaussian(stream_key, dims, width, reach, shards=(), kind=jnp.bfloat16):
    drawn = jax.random.normal(stream_key, dims, jnp.float32) * width
    if len(shards) > 0:
        drawn = steps_of(stream_key, dims, shards, -0.22, 0.18) * drawn
    return jnp.clip(drawn, min=-reach, max=reach).astype(kind)


def setup_inputs(seed: int = 0, part: int = 0) -> dict:
    seeds = jax.random.split(jax.random.key(seed), 10)
    own_keys = jax.random.split(jax.random.fold_in(seeds[9], part), 10)
    return {
        "nodes": gaussian(own_keys[0], (MB, NODES, D), 1.0, 6.0, ((1, 8),)),
        "tile_index": draw_tile_index(jax.random.fold_in(jax.random.fold_in(seeds[9], part), 71), part),
        "tile_values": gaussian(own_keys[2], (TILES, K, TILE, TILE), (K * TILE) ** -0.5, 0.25, ((0, 8),)),
        "halo_rows": draw_halo_rows(jax.random.fold_in(jax.random.fold_in(seeds[9], part), 71), part),
        "w_msg": gaussian(seeds[4], (LAYERS, D, D), D ** -0.5, 0.25, ((0, 2),)),
        "w_in": gaussian(seeds[5], (LAYERS, 2 * D, D), (2 * D) ** -0.5, 0.1875, ((0, 2),)),
        "w_out": gaussian(seeds[6], (LAYERS, D, D), D ** -0.5, 0.25, ((0, 2),)),
        "bias": gaussian(seeds[7], (LAYERS, D), 0.5, 3.0, ((0, 2),), jnp.float32),
        "gain": jnp.clip(1.0 + 0.18 * jax.random.normal(seeds[8], (LAYERS, D), jnp.float32), 0.1, 1.9),
    }


def aggregate(pieces):
    ext, index, values = pieces
    picked = jnp.take(ext, index, axis=1)
    return jnp.einsum('rkij,brkjd->brid', values.astype(jnp.float32), picked.astype(jnp.float32)).astype(jnp.bfloat16)

def reference(nodes, tile_index, tile_values, halo_rows, w_msg, w_in, w_out, bias, gain):
    state = nodes
    slabs = N_SLABX * N_SLABY
    rows_list = halo_rows.reshape(N_SLABX, N_SLABY, 4, HALO)
    grid_x = jnp.arange(N_SLABX, dtype=jnp.int32)[:, None, None, None]
    grid_y = jnp.arange(N_SLABY, dtype=jnp.int32)[None, :, None, None]
    index_s = tile_index.reshape(slabs, TL, K)
    values_s = tile_values.reshape(slabs, TL, K, TILE, TILE)
    for layer in range(LAYERS):
        flat = state.reshape(-1, D)
        msg = jnp.dot(flat, w_msg[layer], preferred_element_type=jnp.float32).astype(jnp.bfloat16)
        msg = msg.reshape(MB, N_SLABX, N_SLABY, NODE_DEV, D)
        sent = msg[:, grid_x, grid_y, rows_list]
        zero_x = jnp.zeros((MB, 1, N_SLABY, HALO, D), jnp.bfloat16)
        zero_y = jnp.zeros((MB, N_SLABX, 1, HALO, D), jnp.bfloat16)
        lower_x = jnp.concatenate([zero_x, sent[:, :-1, :, 0]], axis=1)
        upper_x = jnp.concatenate([sent[:, 1:, :, 1], zero_x], axis=1)
        lower_y = jnp.concatenate([zero_y, sent[:, :, :-1, 2]], axis=2)
        upper_y = jnp.concatenate([sent[:, :, 1:, 3], zero_y], axis=2)
        halos = jnp.stack([lower_x, upper_x, lower_y, upper_y], axis=3)
        local_tiles = msg.reshape(MB, N_SLABX, N_SLABY, TL, TILE, D)
        ext = jnp.concatenate([local_tiles, halos], axis=3)
        ext_s = ext.reshape(MB, slabs, TL + 4, TILE, D).transpose(1, 0, 2, 3, 4)
        agg = lax.map(aggregate, (ext_s, index_s, values_s))
        agg = agg.transpose(1, 0, 2, 3, 4).reshape(-1, D)
        joined = jnp.concatenate([flat, agg], axis=1)
        pre = jnp.dot(joined, w_in[layer], preferred_element_type=jnp.float32) + bias[layer]
        act = jnp.maximum(pre, 0.0).astype(jnp.bfloat16)
        out = jnp.dot(act, w_out[layer], preferred_element_type=jnp.float32)
        mean = lax.optimization_barrier(jnp.mean(out, axis=-1, keepdims=True))
        var = lax.optimization_barrier(jnp.mean(jnp.square(out - mean), axis=-1, keepdims=True))
        normed = (out - mean) / jnp.sqrt(var + 1e-05)
        state = (flat.astype(jnp.float32) + gain[layer] * normed).astype(jnp.bfloat16).reshape(MB, NODES, D)
    return state
```

```python
import functools

import jax
import jax.numpy as jnp
from jax import lax
from jax.experimental import pallas as pl
from jax.experimental.pallas import tpu as pltpu
from jax.sharding import PartitionSpec as P

F32 = jnp.float32
BF16 = jnp.bfloat16
LIMIT = 24 * 1024 * 1024
AXES = ("slabx", "slaby")


def dot(a, b):
    return jnp.dot(a, b, preferred_element_type=F32)


def meetings(sizes):
    return [(axis, turn) for axis in range(2) for turn in range(2) if sizes[axis] > 1 + turn]


def swap(block, axis, turn):
    size = lax.axis_size(AXES[axis])
    route = []
    for low in range(turn, size - 1, 2):
        route += [(low, low + 1), (low + 1, low)]
    return lax.ppermute(block, AXES[axis], route)


def select_rows(halo_ref, rounds, rows):
    picks = []
    for axis, turn in rounds:
        odd = lax.rem(lax.axis_index(AXES[axis]), 2)
        which = 2 * axis + (odd if turn == 0 else 1 - odd)
        listed = halo_ref[0, pl.ds(which, 1), :]
        count = listed.shape[1]
        down = jnp.transpose(jnp.broadcast_to(listed, (count, count)))
        for at in range(0, rows, count):
            columns = lax.broadcasted_iota(jnp.int32, (count, count), 1) + at
            picks.append((down == columns).astype(F32).astype(BF16))
    per = rows // count
    return jnp.concatenate(
        [
            jnp.concatenate(picks[n * per : (n + 1) * per], axis=1)
            for n in range(len(rounds))
        ],
        axis=0,
    )


def pick_kernel(rounds, halo_ref, nodes_ref, state_ref, *rest):
    sends, (sem,) = rest[: len(rounds)], rest[len(rounds) :]
    half, rows, _ = state_ref.shape
    section = lax.axis_index("section")
    fetch = [
        pltpu.make_async_copy(nodes_ref.at[section * half + b], state_ref.at[b], sem.at[b])
        for b in range(half)
    ]
    for copy in fetch:
        copy.start()
    chosen = select_rows(halo_ref, rounds, rows)
    count = chosen.shape[0] // len(rounds)
    for b in range(half):
        fetch[b].wait()
        sent = dot(chosen, state_ref[b]).astype(BF16)
        for n, ref in enumerate(sends):
            ref[b] = sent[n * count : (n + 1) * count]


def local_work(index_ref, values_ref, state, w_in, w_msg, bias, half, base_ref, near_ref, fold_ref):
    tiles, _, tile, _ = values_ref.shape
    width = w_msg.shape[0]
    top, bottom = w_in[:width], w_in[width:]
    fold_ref[...] = dot(w_msg, bottom).astype(BF16)
    for b in range(half):
        base_ref[b] = dot(state[b], top) + bias
        for r in range(tiles):
            other = pl.multiple_of(index_ref[r, 1] * tile, tile)
            pair = jnp.concatenate(
                [state[b, r * tile : (r + 1) * tile, :], state[b, pl.ds(other, tile), :]], axis=0
            )
            edges = jnp.concatenate([values_ref[r, 0], values_ref[r, 1]], axis=1)
            near_ref[b, r * tile : (r + 1) * tile, :] = dot(edges, pair)


def local_kernel(
    layer, index_ref, values_ref, state_ref,
    msg_a, msg_b, in_a, in_b, out_a, out_b, vec_a, vec_b,
    base_ref, near_ref, fold_ref, last_ref, gain_ref,
):
    mine = lax.axis_index("section") == layer
    half = base_ref.shape[0]
    pick = lambda a, b: jnp.where(mine, a[...], b[...])
    vec = pick(vec_a, vec_b)
    gain_ref[...] = vec[1:2]
    last_ref[...] = pick(out_a, out_b)[0]
    local_work(
        index_ref, values_ref, state_ref, pick(in_a, in_b)[0], pick(msg_a, msg_b)[0], vec[0:1],
        half, base_ref, near_ref, fold_ref,
    )


def finish_kernel(
    rounds, final, index_ref, values_ref, halo_ref, state_ref,
    base_ref, near_ref, fold_ref, last_ref, gain_ref, *rest,
):
    recvs, rest = rest[: len(rounds)], rest[len(rounds) :]
    out_ref, rest = rest[0], rest[1:]
    sends, rest = ((), rest) if final else (rest[: len(rounds)], rest[len(rounds) :])
    ext = rest[0]
    half, rows, width = base_ref.shape
    tiles, _, tile, _ = values_ref.shape
    for slot in range(4):
        here = (slot // 2, slot % 2)
        if here in rounds:
            ext[slot] = recvs[rounds.index(here)][...]
        else:
            ext[slot] = jnp.zeros(ext.shape[1:], BF16)

    def slot_of(entry):
        place = entry - tiles
        axis, upper = lax.div(place, 2), lax.rem(place, 2)
        at = jnp.where(axis == 0, lax.axis_index("slabx"), lax.axis_index("slaby"))
        return 2 * axis + 1 - lax.rem(upper + at, 2)

    slots = [[slot_of(index_ref[r, 2]), slot_of(index_ref[r, 3])] for r in range(tiles)]
    chosen = None if final else select_rows(halo_ref, rounds, rows)
    gain = gain_ref[...]
    for b in range(half):
        parts = []
        for r in range(tiles):
            pair = jnp.concatenate([ext[slots[r][0], b], ext[slots[r][1], b]], axis=0)
            edges = jnp.concatenate([values_ref[r, 2], values_ref[r, 3]], axis=1)
            far = dot(edges, pair) + near_ref[b, r * tile : (r + 1) * tile, :]
            parts.append(far.astype(BF16))
        total = jnp.concatenate(parts, axis=0)
        pre = base_ref[b] + dot(total, fold_ref[...])
        act = jnp.maximum(pre, 0.0).astype(BF16)
        out = dot(act, last_ref[...])
        mean = jnp.mean(out, axis=-1, keepdims=True)
        off = out - mean
        var = jnp.mean(off * off, axis=-1, keepdims=True)
        normed = off * lax.rsqrt(var + 1e-05)
        fresh = (state_ref[b].astype(F32) + gain * normed).astype(BF16)
        out_ref[b] = fresh
        if not final:
            sent = dot(chosen, fresh).astype(BF16)
            for n, ref in enumerate(sends):
                ref[b] = sent[n * tile : (n + 1) * tile]


VMEM = pl.BlockSpec(memory_space=pltpu.VMEM)
SMEM = pl.BlockSpec(memory_space=pltpu.SMEM)
HBM = pl.BlockSpec(memory_space=pltpu.HBM)


def shards(nodes, tile_index, tile_values, halo_rows, w_msg, w_in, w_out, bias, gain):
    snaps, rows, width = nodes.shape
    sections = lax.axis_size("section")
    half = snaps // sections
    tiles, _, tile, _ = tile_values.shape
    rounds = meetings([lax.axis_size(name) for name in AXES])
    block = jax.ShapeDtypeStruct((half, tile, width), BF16)
    state_shape = jax.ShapeDtypeStruct((half, rows, width), BF16)
    wide = jax.ShapeDtypeStruct((half, rows, width), F32)
    square = jax.ShapeDtypeStruct((width, width), BF16)
    line = jax.ShapeDtypeStruct((1, width), F32)

    def cost(matmul_rows, nbytes):
        return pl.CostEstimate(
            flops=2 * matmul_rows * width * width, bytes_accessed=nbytes, transcendentals=0
        )

    vec = jnp.concatenate([bias, gain], axis=0)
    mine = (w_msg, w_in, w_out, vec)
    cross = [(0, 1), (1, 0)]
    other = tuple(lax.ppermute(w, "section", cross) for w in mine)

    state, *sends = pl.pallas_call(
        functools.partial(pick_kernel, rounds),
        out_shape=[state_shape] + [block] * len(rounds),
        in_specs=[VMEM, HBM],
        out_specs=[VMEM] * (1 + len(rounds)),
        scratch_shapes=[pltpu.SemaphoreType.DMA((half,))],
        cost_estimate=cost(half * rows, 2 * half * rows * width * 2),
        compiler_params=pltpu.CompilerParams(vmem_limit_bytes=LIMIT),
        name="pick",
    )(halo_rows, nodes)

    for layer in range(2):
        final = layer == 1
        got = [swap(sent, *turn) for sent, turn in zip(sends, rounds)]
        weights = []
        for a, b in zip(mine, other):
            weights += [a, b]
        base, near, fold, last, line_gain = pl.pallas_call(
            functools.partial(local_kernel, layer),
            out_shape=[wide, wide, square, square, line],
            in_specs=[SMEM] + [VMEM] * 10,
            out_specs=[VMEM] * 5,
            cost_estimate=cost(3 * half * rows, 8 * half * rows * width),
            compiler_params=pltpu.CompilerParams(vmem_limit_bytes=LIMIT),
            name=f"local{layer}",
        )(tile_index, tile_values, state, *weights)
        results = pl.pallas_call(
            functools.partial(finish_kernel, rounds, final),
            out_shape=[state_shape] + ([] if final else [block] * len(rounds)),
            in_specs=[SMEM] + [VMEM] * (8 + len(rounds)),
            out_specs=[VMEM] * (1 if final else 1 + len(rounds)),
            scratch_shapes=[pltpu.VMEM((4, half, tile, width), BF16)],
            cost_estimate=cost(3 * half * rows, 8 * half * rows * width),
            compiler_params=pltpu.CompilerParams(vmem_limit_bytes=LIMIT),
            name=f"finish{layer}",
        )(
            tile_index, tile_values, halo_rows, state, base, near, fold, last, line_gain, *got
        )
        state, sends = results[0], results[1:]
    return state


def solution(mesh):
    slab = ("groups", "slabx", "slaby")
    in_specs = (
        P(None, slab, None),
        P(slab, None),
        P(slab, None, None, None),
        P(slab, None, None),
        P("section", None, None),
        P("section", None, None),
        P("section", None, None),
        P("section", None),
        P("section", None),
    )
    out_specs = P("section", slab, None)
    return jax.shard_map(shards, mesh=mesh, in_specs=in_specs, out_specs=out_specs, check_vma=False)
```

```python
import functools

import jax
import jax.numpy as jnp
from jax import lax
from jax.experimental import pallas as pl
from jax.experimental.pallas import tpu as pltpu
from jax.sharding import PartitionSpec as P

F32 = jnp.float32
BF16 = jnp.bfloat16
LIMIT = 24 * 1024 * 1024
AXES = ("slabx", "slaby")


def dot(a, b):
    return jnp.dot(a, b, preferred_element_type=F32)


def meetings(sizes):
    return [(axis, turn) for axis in range(2) for turn in (1, 0) if sizes[axis] > 1 + turn]


def swap(block, axis, turn):
    size = lax.axis_size(AXES[axis])
    route = []
    for low in range(turn, size - 1, 2):
        route += [(low, low + 1), (low + 1, low)]
    return lax.ppermute(block, AXES[axis], route)


def select_rows(halo_ref, rounds, rows):
    picks = []
    for axis, turn in rounds:
        odd = lax.rem(lax.axis_index(AXES[axis]), 2)
        which = 2 * axis + (odd if turn == 0 else 1 - odd)
        listed = halo_ref[0, pl.ds(which, 1), :]
        count = listed.shape[1]
        down = jnp.transpose(jnp.broadcast_to(listed, (count, count)))
        for at in range(0, rows, count):
            columns = lax.broadcasted_iota(jnp.int32, (count, count), 1) + at
            picks.append((down == columns).astype(F32).astype(BF16))
    per = rows // count
    return jnp.concatenate(
        [
            jnp.concatenate(picks[n * per : (n + 1) * per], axis=1)
            for n in range(len(rounds))
        ],
        axis=0,
    )


def pick_kernel(rounds, halo_hbm, nodes_ref, state_ref, *rest):
    sends, (halo_ref, sem) = rest[: len(rounds)], rest[len(rounds) :]
    half, rows, _ = state_ref.shape
    section = lax.axis_index("section")
    lists = pltpu.make_async_copy(halo_hbm, halo_ref, sem.at[half])
    lists.start()
    fetch = [
        pltpu.make_async_copy(nodes_ref.at[section * half + b], state_ref.at[b], sem.at[b])
        for b in range(half)
    ]
    for copy in fetch:
        copy.start()
    lists.wait()
    chosen = select_rows(halo_ref, rounds, rows)
    count = chosen.shape[0] // len(rounds)
    for b in range(half):
        fetch[b].wait()
        sent = dot(chosen, state_ref[b]).astype(BF16)
        for n, ref in enumerate(sends):
            ref[b] = sent[n * count : (n + 1) * count]


def local_kernel(
    layer, index_ref, values_ref, state_ref,
    msg_a, msg_b, in_a, in_b, out_a, out_b, bias_a, bias_b, gain_a, gain_b,
    base_ref, near_ref, fold_ref, last_ref, gain_ref, msg_ref, in_ref, sem,
):
    mine = lax.axis_index("section") == layer
    half = base_ref.shape[0]
    tiles, _, tile, _ = values_ref.shape
    width = last_ref.shape[0]
    into = (msg_ref, in_ref, last_ref)
    kept = [
        pltpu.make_async_copy(w.at[0], ref, sem.at[n])
        for n, (w, ref) in enumerate(zip((msg_a, in_a, out_a), into))
    ]
    came = [
        pltpu.make_async_copy(w.at[0], ref, sem.at[n])
        for n, (w, ref) in enumerate(zip((msg_b, in_b, out_b), into))
    ]

    @pl.when(mine)
    def _():
        for copy in kept:
            copy.start()

    @pl.when(jnp.logical_not(mine))
    def _():
        for copy in came:
            copy.start()

    gain_ref[...] = jnp.where(mine, gain_a[...], gain_b[...])
    bias = jnp.where(mine, bias_a[...], bias_b[...])
    for r in range(tiles):
        other = pl.multiple_of(index_ref[r, 1] * tile, tile)
        edges = jnp.concatenate([values_ref[r, 0], values_ref[r, 1]], axis=1)
        for b in range(half):
            pair = jnp.concatenate(
                [state_ref[b, r * tile : (r + 1) * tile, :], state_ref[b, pl.ds(other, tile), :]],
                axis=0,
            )
            near_ref[b, r * tile : (r + 1) * tile, :] = dot(edges, pair)
    for copy in kept:
        copy.wait()
    fold_ref[...] = dot(msg_ref[...], in_ref[width:]).astype(BF16)
    for b in range(half):
        base_ref[b] = dot(state_ref[b], in_ref[:width]) + bias


def finish_kernel(
    rounds, final, index_ref, values_ref, halo_ref, state_ref,
    base_ref, near_ref, fold_ref, last_ref, gain_ref, *rest,
):
    recvs, rest = rest[: len(rounds)], rest[len(rounds) :]
    out_ref, rest = rest[0], rest[1:]
    sends, rest = ((), rest) if final else (rest[: len(rounds)], rest[len(rounds) :])
    ext, rest = rest[0], rest[1:]
    half, rows, width = base_ref.shape
    tiles, _, tile, _ = values_ref.shape
    for slot in range(4):
        here = (slot // 2, slot % 2)
        if here in rounds:
            ext[slot] = recvs[rounds.index(here)][...]
        else:
            ext[slot] = jnp.zeros(ext.shape[1:], BF16)

    def slot_of(entry):
        place = entry - tiles
        axis, upper = lax.div(place, 2), lax.rem(place, 2)
        at = jnp.where(axis == 0, lax.axis_index("slabx"), lax.axis_index("slaby"))
        return 2 * axis + 1 - lax.rem(upper + at, 2)

    slots = [[slot_of(index_ref[r, 2]), slot_of(index_ref[r, 3])] for r in range(tiles)]
    gain = gain_ref[...]
    acts, outs = [], []
    for b in range(half):
        parts = []
        for r in range(tiles):
            pair = jnp.concatenate([ext[slots[r][0], b], ext[slots[r][1], b]], axis=0)
            edges = jnp.concatenate([values_ref[r, 2], values_ref[r, 3]], axis=1)
            far = dot(edges, pair) + near_ref[b, r * tile : (r + 1) * tile, :]
            parts.append(far.astype(BF16))
        total = jnp.concatenate(parts, axis=0)
        pre = base_ref[b] + dot(total, fold_ref[...])
        acts.append(jnp.maximum(pre, 0.0).astype(BF16))
    for b in range(half):
        outs.append(dot(acts[b], last_ref[...]))
    chosen = None if final else select_rows(halo_ref, rounds, rows)
    writes = []
    for b in range(half):
        out = outs[b]
        mean = jnp.mean(out, axis=-1, keepdims=True)
        off = out - mean
        var = jnp.mean(off * off, axis=-1, keepdims=True)
        normed = off * lax.rsqrt(var + 1e-05)
        fresh = (state_ref[b].astype(F32) + gain * normed).astype(BF16)
        if final:
            done, sem = rest
            done[b] = fresh
            writes.append(pltpu.make_async_copy(done.at[b], out_ref.at[b], sem.at[b]))
            writes[b].start()
        else:
            out_ref[b] = fresh
            sent = dot(chosen, fresh).astype(BF16)
            for n, ref in enumerate(sends):
                ref[b] = sent[n * tile : (n + 1) * tile]
    for copy in writes:
        copy.wait()


VMEM = pl.BlockSpec(memory_space=pltpu.VMEM)
SMEM = pl.BlockSpec(memory_space=pltpu.SMEM)
HBM = pl.BlockSpec(memory_space=pltpu.HBM)


def shards(nodes, tile_index, tile_values, halo_rows, w_msg, w_in, w_out, bias, gain):
    snaps, rows, width = nodes.shape
    sections = lax.axis_size("section")
    half = snaps // sections
    tiles, _, tile, _ = tile_values.shape
    rounds = meetings([lax.axis_size(name) for name in AXES])
    block = jax.ShapeDtypeStruct((half, tile, width), BF16)
    state_shape = jax.ShapeDtypeStruct((half, rows, width), BF16)
    wide = jax.ShapeDtypeStruct((half, rows, width), F32)
    square = jax.ShapeDtypeStruct((width, width), BF16)
    line = jax.ShapeDtypeStruct((1, width), F32)

    def cost(matmul_rows, nbytes):
        return pl.CostEstimate(
            flops=2 * matmul_rows * width * width, bytes_accessed=nbytes, transcendentals=0
        )

    mine = (w_msg, w_in, w_out, bias, gain)
    cross = [(0, 1), (1, 0)]
    other = tuple(lax.ppermute(w, "section", cross) for w in mine)

    state, *sends = pl.pallas_call(
        functools.partial(pick_kernel, rounds),
        out_shape=[state_shape] + [block] * len(rounds),
        in_specs=[HBM, HBM],
        out_specs=[VMEM] * (1 + len(rounds)),
        scratch_shapes=[
            pltpu.VMEM(halo_rows.shape, jnp.int32),
            pltpu.SemaphoreType.DMA((half + 1,)),
        ],
        cost_estimate=cost(half * rows, 2 * half * rows * width * 2),
        compiler_params=pltpu.CompilerParams(vmem_limit_bytes=LIMIT),
        name="pick",
    )(pltpu.with_memory_space_constraint(halo_rows, pltpu.HBM), pltpu.with_memory_space_constraint(nodes, pltpu.HBM))

    for layer in range(2):
        final = layer == 1
        got = [swap(sent, *turn) for sent, turn in zip(sends, rounds)]
        weights = []
        for n, (a, b) in enumerate(zip(mine, other)):
            weights += [pltpu.with_memory_space_constraint(a, pltpu.HBM) if n < 3 else a, b]
        base, near, fold, last, line_gain = pl.pallas_call(
            functools.partial(local_kernel, layer),
            out_shape=[wide, wide, square, square, line],
            in_specs=[SMEM] + [VMEM] * 2 + [HBM, VMEM] * 3 + [VMEM] * 4,
            out_specs=[VMEM] * 5,
            scratch_shapes=[
                pltpu.VMEM((width, width), BF16),
                pltpu.VMEM((2 * width, width), BF16),
                pltpu.SemaphoreType.DMA((3,)),
            ],
            cost_estimate=cost(3 * half * rows, 8 * half * rows * width),
            compiler_params=pltpu.CompilerParams(vmem_limit_bytes=LIMIT),
            name=f"local{layer}",
        )(tile_index, tile_values, state, *weights)
        results = pl.pallas_call(
            functools.partial(finish_kernel, rounds, final),
            out_shape=[state_shape] + ([] if final else [block] * len(rounds)),
            in_specs=[SMEM] + [VMEM] * (8 + len(rounds)),
            out_specs=[HBM] if final else [VMEM] * (1 + len(rounds)),
            scratch_shapes=[pltpu.VMEM((4, half, tile, width), BF16)]
            + (
                [pltpu.VMEM((half, rows, width), BF16), pltpu.SemaphoreType.DMA((half,))]
                if final
                else []
            ),
            cost_estimate=cost(3 * half * rows, 8 * half * rows * width),
            compiler_params=pltpu.CompilerParams(vmem_limit_bytes=LIMIT),
            name=f"finish{layer}",
        )(
            tile_index, tile_values, halo_rows, state, base, near, fold, last, line_gain, *got
        )
        state, sends = results[0], results[1:]
    return state


def solution(mesh):
    slab = ("groups", "slabx", "slaby")
    in_specs = (
        P(None, slab, None),
        P(slab, None),
        P(slab, None, None, None),
        P(slab, None, None),
        P("section", None, None),
        P("section", None, None),
        P("section", None, None),
        P("section", None),
        P("section", None),
    )
    out_specs = P("section", slab, None)
    return jax.shard_map(shards, mesh=mesh, in_specs=in_specs, out_specs=out_specs, check_vma=False)
```

```python
import functools

import jax
import jax.numpy as jnp
from jax import lax
from jax.experimental import pallas as pl
from jax.experimental.pallas import tpu as pltpu
from jax.sharding import PartitionSpec as P

F32 = jnp.float32
BF16 = jnp.bfloat16
LIMIT = 24 * 1024 * 1024
AXES = ("slabx", "slaby")


def dot(a, b):
    return jnp.dot(a, b, preferred_element_type=F32)


def meetings(sizes):
    return [(axis, turn) for turn in range(2) for axis in (1, 0) if sizes[axis] > 1 + turn]


def swap(block, axis, turn):
    names = (AXES[axis], "section")
    size, cores = lax.axis_size(names[0]), lax.axis_size(names[1])
    route = []
    for at in range(size):
        partner = at + 1 if (at + turn) % 2 == 0 else at - 1
        for core in range(cores):
            there = (partner, core) if 0 <= partner < size else (at, cores - 1 - core)
            route.append((at * cores + core, there[0] * cores + there[1]))
    return lax.ppermute(block, names, route)


def select_rows(halo_ref, rounds, rows):
    picks = []
    for axis, turn in rounds:
        odd = lax.rem(lax.axis_index(AXES[axis]), 2)
        which = 2 * axis + (odd if turn == 0 else 1 - odd)
        listed = halo_ref[0, pl.ds(which, 1), :]
        count = listed.shape[1]
        down = jnp.transpose(jnp.broadcast_to(listed, (count, count)))
        for at in range(0, rows, count):
            columns = lax.broadcasted_iota(jnp.int32, (count, count), 1) + at
            picks.append((down == columns).astype(F32).astype(BF16))
    per = rows // count
    return jnp.concatenate(
        [
            jnp.concatenate(picks[n * per : (n + 1) * per], axis=1)
            for n in range(len(rounds))
        ],
        axis=0,
    )


def pick_kernel(rounds, halo_hbm, nodes_ref, bias_hbm, gain_hbm, state_ref, vec_ref, *rest):
    sends, (halo_ref, sem) = rest[: len(rounds)], rest[len(rounds) :]
    half, rows, width = state_ref.shape
    section = lax.axis_index("section")
    lists = pltpu.make_async_copy(halo_hbm, halo_ref, sem.at[half])
    lists.start()
    fetch = [
        pltpu.make_async_copy(nodes_ref.at[section * half + b], state_ref.at[b], sem.at[b])
        for b in range(half)
    ]
    for copy in fetch:
        copy.start()
    lines = [
        pltpu.make_async_copy(line, vec_ref.at[:, pl.ds(n * width, width)], sem.at[half + 1 + n])
        for n, line in enumerate((bias_hbm, gain_hbm))
    ]
    for copy in lines:
        copy.start()
    lists.wait()
    chosen = select_rows(halo_ref, rounds, rows)
    count = chosen.shape[0] // len(rounds)
    for b in range(half):
        fetch[b].wait()
        sent = dot(chosen, state_ref[b]).astype(BF16)
        for n, ref in enumerate(sends):
            ref[b] = sent[n * count : (n + 1) * count]
    for copy in lines:
        copy.wait()


def local_kernel(
    layer, index_ref, values_ref, state_ref,
    msg_a, msg_b, in_a, in_b, out_a, out_b, vec_a, vec_b,
    base_ref, near_ref, fold_ref, last_ref, gain_ref, msg_ref, in_ref, sem,
):
    mine = lax.axis_index("section") == layer
    half = base_ref.shape[0]
    tiles, _, tile, _ = values_ref.shape
    width = last_ref.shape[0]
    into = (msg_ref, in_ref, last_ref)
    kept = [
        pltpu.make_async_copy(w.at[0], ref, sem.at[n])
        for n, (w, ref) in enumerate(zip((msg_a, in_a, out_a), into))
    ]
    came = [
        pltpu.make_async_copy(w.at[0], ref, sem.at[n])
        for n, (w, ref) in enumerate(zip((msg_b, in_b, out_b), into))
    ]

    @pl.when(mine)
    def _():
        for copy in kept:
            copy.start()

    @pl.when(jnp.logical_not(mine))
    def _():
        for copy in came:
            copy.start()

    vec = jnp.where(mine, vec_a[...], vec_b[...])
    bias = vec[:, :width]
    gain_ref[...] = vec[:, width:]
    for r in range(tiles):
        other = pl.multiple_of(index_ref[r, 1] * tile, tile)
        edges = jnp.concatenate([values_ref[r, 0], values_ref[r, 1]], axis=1)
        for b in range(half):
            pair = jnp.concatenate(
                [state_ref[b, r * tile : (r + 1) * tile, :], state_ref[b, pl.ds(other, tile), :]],
                axis=0,
            )
            near_ref[b, r * tile : (r + 1) * tile, :] = dot(edges, pair)
    for copy in kept:
        copy.wait()
    fold_ref[...] = dot(msg_ref[...], in_ref[width:]).astype(BF16)
    for b in range(half):
        base_ref[b] = dot(state_ref[b], in_ref[:width]) + bias


def finish_kernel(
    rounds, final, index_ref, values_ref, halo_ref, state_ref,
    base_ref, near_ref, fold_ref, last_ref, gain_ref, *rest,
):
    recvs, rest = rest[: len(rounds)], rest[len(rounds) :]
    out_ref, rest = rest[0], rest[1:]
    sends, rest = ((), rest) if final else (rest[: len(rounds)], rest[len(rounds) :])
    ext, rest = rest[0], rest[1:]
    half, rows, width = base_ref.shape
    tiles, _, tile, _ = values_ref.shape
    for (axis, turn), recv in zip(rounds, recvs):
        ext[2 * axis + turn] = recv[...]
    ext[4] = jnp.zeros(ext.shape[1:], BF16)

    def slot_of(entry):
        place = entry - tiles
        axis, upper = lax.div(place, 2), lax.rem(place, 2)
        first = axis == 0
        at = jnp.where(first, lax.axis_index(AXES[0]), lax.axis_index(AXES[1]))
        size = jnp.where(first, lax.axis_size(AXES[0]), lax.axis_size(AXES[1]))
        exists = jnp.where(upper == 1, at + 1 < size, at > 0)
        return jnp.where(exists, 2 * axis + 1 - lax.rem(upper + at, 2), 4)

    slots = [[slot_of(index_ref[r, 2]), slot_of(index_ref[r, 3])] for r in range(tiles)]
    gain = gain_ref[...]
    writes = []

    def project(b):
        parts = []
        for r in range(tiles):
            pair = jnp.concatenate([ext[slots[r][0], b], ext[slots[r][1], b]], axis=0)
            edges = jnp.concatenate([values_ref[r, 2], values_ref[r, 3]], axis=1)
            far = dot(edges, pair) + near_ref[b, r * tile : (r + 1) * tile, :]
            parts.append(far.astype(BF16))
        total = jnp.concatenate(parts, axis=0)
        pre = base_ref[b] + dot(total, fold_ref[...])
        return dot(jnp.maximum(pre, 0.0).astype(BF16), last_ref[...])

    def settle(b, out):
        mean = jnp.mean(out, axis=-1, keepdims=True)
        off = out - mean
        var = jnp.mean(off * off, axis=-1, keepdims=True)
        normed = off * lax.rsqrt(var + 1e-05)
        fresh = (state_ref[b].astype(F32) + gain * normed).astype(BF16)
        if final:
            done, sem = rest
            done[b] = fresh
            writes.append(pltpu.make_async_copy(done.at[b], out_ref.at[b], sem.at[b]))
            writes[b].start()
        else:
            out_ref[b] = fresh
        return fresh

    def send(b, fresh):
        sent = dot(chosen, fresh).astype(BF16)
        for n, ref in enumerate(sends):
            ref[b] = sent[n * tile : (n + 1) * tile]

    chosen = None if final else select_rows(halo_ref, rounds, rows)
    outs = [project(0)]
    for b in range(half):
        if b + 1 < half:
            outs.append(project(b + 1))
        fresh = settle(b, outs[b])
        if not final:
            send(b, fresh)
    for copy in writes:
        copy.wait()


VMEM = pl.BlockSpec(memory_space=pltpu.VMEM)
SMEM = pl.BlockSpec(memory_space=pltpu.SMEM)
HBM = pl.BlockSpec(memory_space=pltpu.HBM)


def shards(nodes, tile_index, tile_values, halo_rows, w_msg, w_in, w_out, bias, gain):
    snaps, rows, width = nodes.shape
    sections = lax.axis_size("section")
    half = snaps // sections
    tiles, _, tile, _ = tile_values.shape
    rounds = meetings([lax.axis_size(name) for name in AXES])
    block = jax.ShapeDtypeStruct((half, tile, width), BF16)
    state_shape = jax.ShapeDtypeStruct((half, rows, width), BF16)
    wide = jax.ShapeDtypeStruct((half, rows, width), F32)
    square = jax.ShapeDtypeStruct((width, width), BF16)
    line = jax.ShapeDtypeStruct((1, width), F32)
    vec_shape = jax.ShapeDtypeStruct((1, 2 * width), F32)

    def cost(matmul_rows, nbytes):
        return pl.CostEstimate(
            flops=2 * matmul_rows * width * width, bytes_accessed=nbytes, transcendentals=0
        )

    mine = (w_msg, w_in, w_out)
    cross = [(0, 1), (1, 0)]
    in_hbm = lambda a: pltpu.with_memory_space_constraint(a, pltpu.HBM)
    other = tuple(lax.ppermute(w, "section", cross) for w in mine)

    state, vec, *sends = pl.pallas_call(
        functools.partial(pick_kernel, rounds),
        out_shape=[state_shape, vec_shape] + [block] * len(rounds),
        in_specs=[HBM] * 4,
        out_specs=[VMEM] * (2 + len(rounds)),
        scratch_shapes=[
            pltpu.VMEM(halo_rows.shape, jnp.int32),
            pltpu.SemaphoreType.DMA((half + 3,)),
        ],
        cost_estimate=cost(half * rows, 2 * half * rows * width * 2),
        compiler_params=pltpu.CompilerParams(vmem_limit_bytes=LIMIT),
        name="pick",
    )(*(in_hbm(a) for a in (halo_rows, nodes, bias, gain)))
    swapped = lax.ppermute(vec, "section", cross)

    for layer in range(2):
        final = layer == 1
        got = [swap(sent, *turn) for sent, turn in zip(sends, rounds)]
        weights = []
        for a, b in zip(mine, other):
            weights += [in_hbm(a), b]
        weights += [vec, swapped]
        base, near, fold, last, line_gain = pl.pallas_call(
            functools.partial(local_kernel, layer),
            out_shape=[wide, wide, square, square, line],
            in_specs=[SMEM] + [VMEM] * 2 + [HBM, VMEM] * 3 + [VMEM] * 2,
            out_specs=[VMEM] * 5,
            scratch_shapes=[
                pltpu.VMEM((width, width), BF16),
                pltpu.VMEM((2 * width, width), BF16),
                pltpu.SemaphoreType.DMA((3,)),
            ],
            cost_estimate=cost(3 * half * rows, 8 * half * rows * width),
            compiler_params=pltpu.CompilerParams(vmem_limit_bytes=LIMIT),
            name=f"local{layer}",
        )(tile_index, tile_values, state, *weights)
        results = pl.pallas_call(
            functools.partial(finish_kernel, rounds, final),
            out_shape=[state_shape] + ([] if final else [block] * len(rounds)),
            in_specs=[SMEM] + [VMEM] * (8 + len(rounds)),
            out_specs=[HBM] if final else [VMEM] * (1 + len(rounds)),
            scratch_shapes=[pltpu.VMEM((5, half, tile, width), BF16)]
            + (
                [pltpu.VMEM((half, rows, width), BF16), pltpu.SemaphoreType.DMA((half,))]
                if final
                else []
            ),
            cost_estimate=cost(3 * half * rows, 8 * half * rows * width),
            compiler_params=pltpu.CompilerParams(vmem_limit_bytes=LIMIT),
            name=f"finish{layer}",
        )(
            tile_index, tile_values, halo_rows, state, base, near, fold, last, line_gain, *got
        )
        state, sends = results[0], results[1:]
    return state


def solution(mesh):
    slab = ("groups", "slabx", "slaby")
    in_specs = (
        P(None, slab, None),
        P(slab, None),
        P(slab, None, None, None),
        P(slab, None, None),
        P("section", None, None),
        P("section", None, None),
        P("section", None, None),
        P("section", None),
        P("section", None),
    )
    out_specs = P("section", slab, None)
    return jax.shard_map(shards, mesh=mesh, in_specs=in_specs, out_specs=out_specs, check_vma=False)
```

```python
import functools

import jax
import jax.numpy as jnp
from jax import lax
from jax.experimental import pallas as pl
from jax.experimental.pallas import tpu as pltpu
from jax.sharding import PartitionSpec as P

F32 = jnp.float32
BF16 = jnp.bfloat16
LIMIT = 24 * 1024 * 1024
AXES = ("slabx", "slaby")


def dot(a, b):
    return jnp.dot(a, b, preferred_element_type=F32)


def meetings(sizes):
    return [(axis, turn) for turn in range(2) for axis in (1, 0) if sizes[axis] > 1 + turn]


def swap(block, axis, turn):
    names = (AXES[axis], "section")
    size, cores = lax.axis_size(names[0]), lax.axis_size(names[1])
    route = []
    for at in range(size):
        partner = at + 1 if (at + turn) % 2 == 0 else at - 1
        for core in range(cores):
            there = (partner, core) if 0 <= partner < size else (at, cores - 1 - core)
            route.append((at * cores + core, there[0] * cores + there[1]))
    return lax.ppermute(block, names, route)


def select_rows(halo_ref, rounds, rows):
    picks = []
    for axis, turn in rounds:
        odd = lax.rem(lax.axis_index(AXES[axis]), 2)
        which = 2 * axis + (odd if turn == 0 else 1 - odd)
        listed = halo_ref[0, pl.ds(which, 1), :]
        count = listed.shape[1]
        down = jnp.transpose(jnp.broadcast_to(listed, (count, count)))
        for at in range(0, rows, count):
            columns = lax.broadcasted_iota(jnp.int32, (count, count), 1) + at
            picks.append((down == columns).astype(F32).astype(BF16))
    per = rows // count
    return jnp.concatenate(
        [
            jnp.concatenate(picks[n * per : (n + 1) * per], axis=1)
            for n in range(len(rounds))
        ],
        axis=0,
    )


def pick_kernel(rounds, half, halo_hbm, nodes_ref, bias_hbm, gain_hbm, *rest):
    weights, rest = rest[:3], rest[3:]
    states, rest = rest[:half], rest[half:]
    vec_ref, kept, rest = rest[0], rest[1:4], rest[4:]
    sends, (halo_ref, sem) = rest[: half * len(rounds)], rest[half * len(rounds) :]
    rows, width = states[0].shape
    section = lax.axis_index("section")
    lists = pltpu.make_async_copy(halo_hbm, halo_ref, sem.at[0])
    lists.start()
    fetch = [
        pltpu.make_async_copy(nodes_ref.at[section * half + b], states[b], sem.at[1 + b])
        for b in range(half)
    ]
    lines = [
        pltpu.make_async_copy(line, vec_ref.at[:, pl.ds(n * width, width)], sem.at[half + 1 + n])
        for n, line in enumerate((bias_hbm, gain_hbm))
    ]
    lines += [
        pltpu.make_async_copy(w.at[0], ref, sem.at[half + 3 + n])
        for n, (w, ref) in enumerate(zip(weights, kept))
    ]
    for copy in fetch + lines:
        copy.start()
    lists.wait()
    chosen = select_rows(halo_ref, rounds, rows)
    count = chosen.shape[0] // len(rounds)
    for b in range(half):
        fetch[b].wait()
        sent = dot(chosen, states[b][...]).astype(BF16)
        for n in range(len(rounds)):
            sends[b * len(rounds) + n][...] = sent[n * count : (n + 1) * count]
    for copy in lines:
        copy.wait()


def local_kernel(layer, prepare, half, index_ref, values_ref, *rest):
    states, rest = rest[:half], rest[half:]
    msg_a, in_a, out_a, vec_a, msg_b, in_b, out_b, vec_b = rest[:8]
    bases, rest = rest[8 : 8 + half], rest[8 + half :]
    nears, rest = rest[:half], rest[half:]
    mine = lax.axis_index("section") == layer
    tiles, _, tile, _ = values_ref.shape
    width = msg_a.shape[-1]
    for r in range(tiles):
        other = pl.multiple_of(index_ref[r, 1] * tile, tile)
        edges = jnp.concatenate([values_ref[r, 0], values_ref[r, 1]], axis=1)
        for state, near in zip(states, nears):
            pair = jnp.concatenate(
                [state[r * tile : (r + 1) * tile, :], state[pl.ds(other, tile), :]], axis=0
            )
            near[r * tile : (r + 1) * tile, :] = dot(edges, pair)
    vec = jnp.where(mine, vec_a[...], vec_b[...])
    bias = vec[:, :width]
    if prepare:
        fold_ref, last_ref, gain_ref = rest
        gain_ref[...] = vec[:, width:]

    def work(msg, into, out):
        if prepare:
            last_ref[...] = out()
            fold_ref[...] = dot(msg(), into(width)).astype(BF16)
        for state, base in zip(states, bases):
            base[...] = dot(state[...], into(0)) + bias

    @pl.when(mine)
    def _():
        work(lambda: msg_a[...], lambda at: in_a[at : at + width], lambda: out_a[...])

    @pl.when(jnp.logical_not(mine))
    def _():
        work(lambda: msg_b[0], lambda at: in_b[0, at : at + width], lambda: out_b[0])


def finish_kernel(rounds, last_layer, final, earlier, index_ref, values_ref, halo_ref, state_ref, *rest):
    base_ref, near_ref, fold_ref, last_ref, gain_ref = rest[:5]
    recvs, rest = rest[5 : 5 + len(rounds)], rest[5 + len(rounds) :]
    before, rest = rest[:earlier], rest[earlier:]
    out_ref, rest = rest[0], rest[1:]
    sends, rest = ((), rest) if last_layer else (rest[: len(rounds)], rest[len(rounds) :])
    ext, rest = rest[0], rest[1:]
    rows, width = base_ref.shape
    tiles, _, tile, _ = values_ref.shape
    writes = []
    for n, ready in enumerate(before):
        writes.append(pltpu.make_async_copy(ready, out_ref.at[n], rest[1].at[n]))
        writes[n].start()
    for (axis, turn), recv in zip(rounds, recvs):
        ext[2 * axis + turn] = recv[...]
    ext[4] = jnp.zeros(ext.shape[1:], BF16)

    def slot_of(entry):
        place = entry - tiles
        axis, upper = lax.div(place, 2), lax.rem(place, 2)
        first = axis == 0
        at = jnp.where(first, lax.axis_index(AXES[0]), lax.axis_index(AXES[1]))
        size = jnp.where(first, lax.axis_size(AXES[0]), lax.axis_size(AXES[1]))
        exists = jnp.where(upper == 1, at + 1 < size, at > 0)
        return jnp.where(exists, 2 * axis + 1 - lax.rem(upper + at, 2), 4)

    parts = []
    for r in range(tiles):
        pair = jnp.concatenate(
            [ext[slot_of(index_ref[r, 2])], ext[slot_of(index_ref[r, 3])]], axis=0
        )
        edges = jnp.concatenate([values_ref[r, 2], values_ref[r, 3]], axis=1)
        far = dot(edges, pair) + near_ref[r * tile : (r + 1) * tile, :]
        parts.append(far.astype(BF16))
    pre = base_ref[...] + dot(jnp.concatenate(parts, axis=0), fold_ref[...])
    out = dot(jnp.maximum(pre, 0.0).astype(BF16), last_ref[...])
    mean = jnp.mean(out, axis=-1, keepdims=True)
    off = out - mean
    var = jnp.mean(off * off, axis=-1, keepdims=True)
    normed = off * lax.rsqrt(var + 1e-05)
    fresh = (state_ref[...].astype(F32) + gain_ref[...] * normed).astype(BF16)
    if final:
        done, sem = rest
        done[...] = fresh
        writes.append(pltpu.make_async_copy(done, out_ref.at[earlier], sem.at[earlier]))
        writes[earlier].start()
    else:
        out_ref[...] = fresh
    if sends:
        sent = dot(select_rows(halo_ref, rounds, rows), fresh).astype(BF16)
        for n, ref in enumerate(sends):
            ref[...] = sent[n * tile : (n + 1) * tile]
    for copy in writes:
        copy.wait()


VMEM = pl.BlockSpec(memory_space=pltpu.VMEM)
SMEM = pl.BlockSpec(memory_space=pltpu.SMEM)
HBM = pl.BlockSpec(memory_space=pltpu.HBM)


def shards(nodes, tile_index, tile_values, halo_rows, w_msg, w_in, w_out, bias, gain):
    snaps, rows, width = nodes.shape
    sections = lax.axis_size("section")
    half = snaps // sections
    tiles, _, tile, _ = tile_values.shape
    rounds = meetings([lax.axis_size(name) for name in AXES])
    block = jax.ShapeDtypeStruct((tile, width), BF16)
    plane = jax.ShapeDtypeStruct((rows, width), BF16)
    wide = jax.ShapeDtypeStruct((rows, width), F32)
    square = jax.ShapeDtypeStruct((width, width), BF16)
    line = jax.ShapeDtypeStruct((1, width), F32)
    swaps = len(rounds)
    params = pltpu.CompilerParams(vmem_limit_bytes=LIMIT)
    in_hbm = lambda a: pltpu.with_memory_space_constraint(a, pltpu.HBM)

    def cost(matmul_rows):
        return pl.CostEstimate(
            flops=2 * matmul_rows * width * width,
            bytes_accessed=4 * matmul_rows * width,
            transcendentals=0,
        )

    mine = (w_msg, w_in, w_out)
    cross = [(0, 1), (1, 0)]
    other = tuple(lax.ppermute(w, "section", cross) for w in mine)
    picked = pl.pallas_call(
        functools.partial(pick_kernel, rounds, half),
        out_shape=[plane] * half
        + [jax.ShapeDtypeStruct((1, 2 * width), F32)]
        + [jax.ShapeDtypeStruct(w.shape[1:], BF16) for w in mine]
        + [block] * (half * swaps),
        in_specs=[HBM] * 7,
        out_specs=[VMEM] * (half + 4 + half * swaps),
        scratch_shapes=[
            pltpu.VMEM(halo_rows.shape, jnp.int32),
            pltpu.SemaphoreType.DMA((half + 6,)),
        ],
        cost_estimate=cost(half * rows),
        compiler_params=params,
        name="pick",
    )(*(in_hbm(a) for a in (halo_rows, nodes, bias, gain) + mine))
    states, vec, kept = picked[:half], picked[half], picked[half + 1 : half + 4]
    sends = [picked[half + 4 + b * swaps : half + 4 + (b + 1) * swaps] for b in range(half)]
    weights = (*kept, vec, *other, lax.ppermute(vec, "section", cross))

    def local(layer, prepare, chosen):
        count = len(chosen)
        results = pl.pallas_call(
            functools.partial(local_kernel, layer, prepare, count),
            out_shape=[wide] * (2 * count) + ([square, square, line] if prepare else []),
            in_specs=[SMEM] + [VMEM] * (9 + count),
            out_specs=[VMEM] * (2 * count + (3 if prepare else 0)),
            cost_estimate=cost(2 * count * rows + (width if prepare else 0)),
            compiler_params=params,
            name=f"local{layer}",
        )(tile_index, tile_values, *chosen, *weights)
        return results[:count], results[count : 2 * count], results[2 * count :]

    for layer in range(2):
        final = layer == 1
        got = [[swap(sent, *turn) for sent, turn in zip(sends[b], rounds)] for b in range(half)]
        if final:
            parts = [local(layer, b == 0, states[b : b + 1]) for b in range(half)]
            bases, nears = [p[0][0] for p in parts], [p[1][0] for p in parts]
            shared = parts[0][2]
        else:
            bases, nears, shared = local(layer, True, states)
        fresh, sends = [], []
        for b in range(half):
            ending = final and b == half - 1
            before = fresh if ending else []
            scratch = [pltpu.VMEM((5, tile, width), BF16)]
            if ending:
                scratch += [pltpu.VMEM((rows, width), BF16), pltpu.SemaphoreType.DMA((half,))]
            results = pl.pallas_call(
                functools.partial(finish_kernel, rounds, final, ending, len(before)),
                out_shape=[jax.ShapeDtypeStruct((half, rows, width), BF16) if ending else plane]
                + ([] if final else [block] * swaps),
                in_specs=[SMEM] + [VMEM] * (8 + swaps + len(before)),
                out_specs=[HBM if ending else VMEM] + ([] if final else [VMEM] * swaps),
                scratch_shapes=scratch,
                cost_estimate=cost((3 if final else 4) * rows),
                compiler_params=params,
                name=f"finish{layer}",
            )(
                tile_index, tile_values, halo_rows, states[b], bases[b], nears[b], *shared,
                *got[b], *before,
            )
            fresh.append(results[0])
            sends.append(results[1:])
        states = fresh
    return states[-1]


def solution(mesh):
    slab = ("groups", "slabx", "slaby")
    in_specs = (
        P(None, slab, None),
        P(slab, None),
        P(slab, None, None, None),
        P(slab, None, None),
        P("section", None, None),
        P("section", None, None),
        P("section", None, None),
        P("section", None),
        P("section", None),
    )
    out_specs = P("section", slab, None)
    return jax.shard_map(shards, mesh=mesh, in_specs=in_specs, out_specs=out_specs, check_vma=False)
```

```python
import functools

import jax
import jax.numpy as jnp
from jax import lax
from jax.experimental import pallas as pl
from jax.experimental.pallas import tpu as pltpu
from jax.sharding import PartitionSpec as P

F32 = jnp.float32
BF16 = jnp.bfloat16
LIMIT = 24 * 1024 * 1024
AXES = ("slabx", "slaby")


def dot(a, b):
    return jnp.dot(a, b, preferred_element_type=F32)


def meetings(sizes):
    return [(axis, turn) for turn in range(2) for axis in (1, 0) if sizes[axis] > 1 + turn]


def swap(block, axis, turn):
    names = (AXES[axis], "section")
    size, cores = lax.axis_size(names[0]), lax.axis_size(names[1])
    route = []
    for at in range(size):
        partner = at + 1 if (at + turn) % 2 == 0 else at - 1
        for core in range(cores):
            there = (partner, core) if 0 <= partner < size else (at, cores - 1 - core)
            route.append((at * cores + core, there[0] * cores + there[1]))
    return lax.ppermute(block, names, route)


def select_rows(halo_ref, rounds, rows):
    picks = []
    for axis, turn in rounds:
        odd = lax.rem(lax.axis_index(AXES[axis]), 2)
        which = 2 * axis + (odd if turn == 0 else 1 - odd)
        listed = halo_ref[0, pl.ds(which, 1), :]
        count = listed.shape[1]
        down = jnp.transpose(jnp.broadcast_to(listed, (count, count)))
        for at in range(0, rows, count):
            columns = lax.broadcasted_iota(jnp.int32, (count, count), 1) + at
            picks.append((down == columns).astype(F32).astype(BF16))
    per = rows // count
    return jnp.concatenate(
        [
            jnp.concatenate(picks[n * per : (n + 1) * per], axis=1)
            for n in range(len(rounds))
        ],
        axis=0,
    )


def pick_kernel(rounds, half, halo_hbm, nodes_ref, bias_hbm, gain_hbm, *rest):
    weights, rest = rest[:3], rest[3:]
    states, rest = rest[:half], rest[half:]
    vec_ref, kept, rest = rest[0], rest[1:4], rest[4:]
    sends, (halo_ref, sem) = rest[: half * len(rounds)], rest[half * len(rounds) :]
    rows, width = states[0].shape
    section = lax.axis_index("section")
    lists = pltpu.make_async_copy(halo_hbm, halo_ref, sem.at[0])
    lists.start()
    fetch = [
        pltpu.make_async_copy(nodes_ref.at[section * half + b], states[b], sem.at[1 + b])
        for b in range(half)
    ]
    lines = [
        pltpu.make_async_copy(line, vec_ref.at[:, pl.ds(n * width, width)], sem.at[half + 1 + n])
        for n, line in enumerate((bias_hbm, gain_hbm))
    ]
    lines += [
        pltpu.make_async_copy(w.at[0], ref, sem.at[half + 3 + n])
        for n, (w, ref) in enumerate(zip(weights, kept))
    ]
    for copy in fetch + lines:
        copy.start()
    lists.wait()
    chosen = select_rows(halo_ref, rounds, rows)
    count = chosen.shape[0] // len(rounds)
    for b in range(half):
        fetch[b].wait()
        sent = dot(chosen, states[b][...]).astype(BF16)
        for n in range(len(rounds)):
            sends[b * len(rounds) + n][...] = sent[n * count : (n + 1) * count]
    for copy in lines:
        copy.wait()


def local_kernel(layer, prepare, half, index_ref, values_ref, *rest):
    states, rest = rest[:half], rest[half:]
    msg_a, in_a, out_a, vec_a, msg_b, in_b, out_b, vec_b = rest[:8]
    bases, rest = rest[8 : 8 + half], rest[8 + half :]
    nears, rest = rest[:half], rest[half:]
    mine = lax.axis_index("section") == layer
    tiles, _, tile, _ = values_ref.shape
    width = msg_a.shape[-1]
    for r in range(tiles):
        other = pl.multiple_of(index_ref[r, 1] * tile, tile)
        edges = jnp.concatenate([values_ref[r, 0], values_ref[r, 1]], axis=1)
        for state, near in zip(states, nears):
            pair = jnp.concatenate(
                [state[r * tile : (r + 1) * tile, :], state[pl.ds(other, tile), :]], axis=0
            )
            near[r * tile : (r + 1) * tile, :] = dot(edges, pair)
    vec = jnp.where(mine, vec_a[...], vec_b[...])
    bias = vec[:, :width]
    if prepare:
        fold_ref, last_ref, gain_ref = rest
        gain_ref[...] = vec[:, width:]

    def work(msg, into, out):
        if prepare:
            whole = out().astype(F32)
            last_ref[...] = (whole - jnp.mean(whole, axis=-1, keepdims=True)).astype(BF16)
            fold_ref[...] = dot(msg(), into(width)).astype(BF16)
        for state, base in zip(states, bases):
            base[...] = dot(state[...], into(0)) + bias

    @pl.when(mine)
    def _():
        work(lambda: msg_a[...], lambda at: in_a[at : at + width], lambda: out_a[...])

    @pl.when(jnp.logical_not(mine))
    def _():
        work(lambda: msg_b[0], lambda at: in_b[0, at : at + width], lambda: out_b[0])


def finish_kernel(rounds, last_layer, final, earlier, index_ref, values_ref, halo_ref, state_ref, *rest):
    base_ref, near_ref, fold_ref, last_ref, gain_ref = rest[:5]
    recvs, rest = rest[5 : 5 + len(rounds)], rest[5 + len(rounds) :]
    before, rest = rest[:earlier], rest[earlier:]
    out_ref, rest = rest[0], rest[1:]
    sends, rest = ((), rest) if last_layer else (rest[: len(rounds)], rest[len(rounds) :])
    ext, rest = rest[0], rest[1:]
    rows, width = base_ref.shape
    tiles, _, tile, _ = values_ref.shape
    writes = []
    for n, ready in enumerate(before):
        writes.append(pltpu.make_async_copy(ready, out_ref.at[n], rest[1].at[n]))
        writes[n].start()
    for (axis, turn), recv in zip(rounds, recvs):
        ext[2 * axis + turn] = recv[...]
    ext[4] = jnp.zeros(ext.shape[1:], BF16)

    def slot_of(entry):
        place = entry - tiles
        axis, upper = lax.div(place, 2), lax.rem(place, 2)
        first = axis == 0
        at = jnp.where(first, lax.axis_index(AXES[0]), lax.axis_index(AXES[1]))
        size = jnp.where(first, lax.axis_size(AXES[0]), lax.axis_size(AXES[1]))
        exists = jnp.where(upper == 1, at + 1 < size, at > 0)
        return jnp.where(exists, 2 * axis + 1 - lax.rem(upper + at, 2), 4)

    if sends:
        chosen = select_rows(halo_ref, rounds, rows)
    fresh = []
    for low, high in ((0, tiles - 1), (tiles - 1, tiles)):
        at = pl.ds(low * tile, (high - low) * tile)
        parts = []
        for r in range(low, high):
            pair = jnp.concatenate(
                [ext[slot_of(index_ref[r, 2])], ext[slot_of(index_ref[r, 3])]], axis=0
            )
            edges = jnp.concatenate([values_ref[r, 2], values_ref[r, 3]], axis=1)
            far = dot(edges, pair) + near_ref[r * tile : (r + 1) * tile, :]
            parts.append(far.astype(BF16))
        pre = base_ref[at, :] + dot(jnp.concatenate(parts, axis=0), fold_ref[...])
        off = dot(jnp.maximum(pre, 0.0).astype(BF16), last_ref[...])
        var = jnp.mean(off * off, axis=-1, keepdims=True)
        normed = off * lax.rsqrt(var + 1e-05)
        fresh.append((state_ref[at, :].astype(F32) + gain_ref[...] * normed).astype(BF16))
        if final:
            done, sem = rest
            done[at, :] = fresh[-1]
            writes.append(
                pltpu.make_async_copy(
                    done.at[at, :], out_ref.at[earlier, at, :], sem.at[len(writes)]
                )
            )
            writes[-1].start()
        else:
            out_ref[at, :] = fresh[-1]
    if sends:
        early = (tiles - 1) * tile
        sent = dot(chosen[:, :early], fresh[0])
        sent = (sent + dot(chosen[:, early:], fresh[-1])).astype(BF16)
        for n, ref in enumerate(sends):
            ref[...] = sent[n * tile : (n + 1) * tile]
    for copy in writes:
        copy.wait()


VMEM = pl.BlockSpec(memory_space=pltpu.VMEM)
SMEM = pl.BlockSpec(memory_space=pltpu.SMEM)
HBM = pl.BlockSpec(memory_space=pltpu.HBM)


def shards(nodes, tile_index, tile_values, halo_rows, w_msg, w_in, w_out, bias, gain):
    snaps, rows, width = nodes.shape
    sections = lax.axis_size("section")
    half = snaps // sections
    tiles, _, tile, _ = tile_values.shape
    rounds = meetings([lax.axis_size(name) for name in AXES])
    block = jax.ShapeDtypeStruct((tile, width), BF16)
    plane = jax.ShapeDtypeStruct((rows, width), BF16)
    wide = jax.ShapeDtypeStruct((rows, width), F32)
    square = jax.ShapeDtypeStruct((width, width), BF16)
    line = jax.ShapeDtypeStruct((1, width), F32)
    swaps = len(rounds)
    params = pltpu.CompilerParams(vmem_limit_bytes=LIMIT)
    in_hbm = lambda a: pltpu.with_memory_space_constraint(a, pltpu.HBM)

    def cost(matmul_rows):
        return pl.CostEstimate(
            flops=2 * matmul_rows * width * width,
            bytes_accessed=4 * matmul_rows * width,
            transcendentals=0,
        )

    mine = (w_msg, w_in, w_out)
    cross = [(0, 1), (1, 0)]
    other = tuple(lax.ppermute(w, "section", cross) for w in mine)
    picked = pl.pallas_call(
        functools.partial(pick_kernel, rounds, half),
        out_shape=[plane] * half
        + [jax.ShapeDtypeStruct((1, 2 * width), F32)]
        + [jax.ShapeDtypeStruct(w.shape[1:], BF16) for w in mine]
        + [block] * (half * swaps),
        in_specs=[HBM] * 7,
        out_specs=[VMEM] * (half + 4 + half * swaps),
        scratch_shapes=[
            pltpu.VMEM(halo_rows.shape, jnp.int32),
            pltpu.SemaphoreType.DMA((half + 6,)),
        ],
        cost_estimate=cost(half * rows),
        compiler_params=params,
        name="pick",
    )(*(in_hbm(a) for a in (halo_rows, nodes, bias, gain) + mine))
    states, vec, kept = picked[:half], picked[half], picked[half + 1 : half + 4]
    sends = [picked[half + 4 + b * swaps : half + 4 + (b + 1) * swaps] for b in range(half)]
    weights = (*kept, vec, *other, lax.ppermute(vec, "section", cross))

    def local(layer, prepare, chosen):
        count = len(chosen)
        results = pl.pallas_call(
            functools.partial(local_kernel, layer, prepare, count),
            out_shape=[wide] * (2 * count) + ([square, square, line] if prepare else []),
            in_specs=[SMEM] + [VMEM] * (9 + count),
            out_specs=[VMEM] * (2 * count + (3 if prepare else 0)),
            cost_estimate=cost(2 * count * rows + (width if prepare else 0)),
            compiler_params=params,
            name=f"local{layer}",
        )(tile_index, tile_values, *chosen, *weights)
        return results[:count], results[count : 2 * count], results[2 * count :]

    for layer in range(2):
        final = layer == 1
        bases, nears, shared = local(layer, True, states)
        if not final:
            bases, sends[1:] = lax.optimization_barrier((bases, sends[1:]))
        got = [[swap(sent, *turn) for sent, turn in zip(sends[b], rounds)] for b in range(half)]
        fresh, sends = [], []
        for b in range(half):
            ending = final and b == half - 1
            before = fresh if ending else []
            scratch = [pltpu.VMEM((5, tile, width), BF16)]
            if ending:
                scratch += [pltpu.VMEM((rows, width), BF16), pltpu.SemaphoreType.DMA((half + 1,))]
            results = pl.pallas_call(
                functools.partial(finish_kernel, rounds, final, ending, len(before)),
                out_shape=[jax.ShapeDtypeStruct((half, rows, width), BF16) if ending else plane]
                + ([] if final else [block] * swaps),
                in_specs=[SMEM] + [VMEM] * (8 + swaps + len(before)),
                out_specs=[HBM if ending else VMEM] + ([] if final else [VMEM] * swaps),
                scratch_shapes=scratch,
                cost_estimate=cost((3 if final else 4) * rows),
                compiler_params=params,
                name=f"finish{layer}",
            )(
                tile_index, tile_values, halo_rows, states[b], bases[b], nears[b], *shared,
                *got[b], *before,
            )
            fresh.append(results[0])
            sends.append(results[1:])
        states = fresh
    return states[-1]


def solution(mesh):
    slab = ("groups", "slabx", "slaby")
    in_specs = (
        P(None, slab, None),
        P(slab, None),
        P(slab, None, None, None),
        P(slab, None, None),
        P("section", None, None),
        P("section", None, None),
        P("section", None, None),
        P("section", None),
        P("section", None),
    )
    out_specs = P("section", slab, None)
    return jax.shard_map(shards, mesh=mesh, in_specs=in_specs, out_specs=out_specs, check_vma=False)
```

```python
import functools

import jax
import jax.numpy as jnp
from jax import lax
from jax.experimental import pallas as pl
from jax.experimental.pallas import tpu as pltpu
from jax.sharding import PartitionSpec as P

F32 = jnp.float32
BF16 = jnp.bfloat16
LIMIT = 24 * 1024 * 1024
AXES = ("slabx", "slaby")


def dot(a, b):
    return jnp.dot(a, b, preferred_element_type=F32)


def meetings(sizes):
    return [(axis, turn) for turn in range(2) for axis in (1, 0) if sizes[axis] > 1 + turn]


def swap(block, axis, turn):
    names = (AXES[axis], "section")
    size, cores = lax.axis_size(names[0]), lax.axis_size(names[1])
    route = []
    for at in range(size):
        partner = at + 1 if (at + turn) % 2 == 0 else at - 1
        for core in range(cores):
            there = (partner, core) if 0 <= partner < size else (at, cores - 1 - core)
            route.append((at * cores + core, there[0] * cores + there[1]))
    return lax.ppermute(block, names, route)


def select_rows(halo_ref, rounds, rows):
    picks = []
    for axis, turn in rounds:
        odd = lax.rem(lax.axis_index(AXES[axis]), 2)
        which = 2 * axis + (odd if turn == 0 else 1 - odd)
        listed = halo_ref[0, pl.ds(which, 1), :]
        count = listed.shape[1]
        down = jnp.transpose(jnp.broadcast_to(listed, (count, count)))
        for at in range(0, rows, count):
            columns = lax.broadcasted_iota(jnp.int32, (count, count), 1) + at
            picks.append((down == columns).astype(F32).astype(BF16))
    per = rows // count
    return jnp.concatenate(
        [
            jnp.concatenate(picks[n * per : (n + 1) * per], axis=1)
            for n in range(len(rounds))
        ],
        axis=0,
    )


def pick_kernel(rounds, half, halo_hbm, nodes_ref, bias_hbm, gain_hbm, *rest):
    weights, rest = rest[:3], rest[3:]
    states, rest = rest[:half], rest[half:]
    vec_ref, kept, rest = rest[0], rest[1:4], rest[4:]
    sends, (halo_ref, sem) = rest[: half * len(rounds)], rest[half * len(rounds) :]
    rows, width = states[0].shape
    section = lax.axis_index("section")
    lists = pltpu.make_async_copy(halo_hbm, halo_ref, sem.at[0])
    lists.start()
    fetch = [
        pltpu.make_async_copy(nodes_ref.at[section * half + b], states[b], sem.at[1 + b])
        for b in range(half)
    ]
    lines = [
        pltpu.make_async_copy(line, vec_ref.at[:, pl.ds(n * width, width)], sem.at[half + 1 + n])
        for n, line in enumerate((bias_hbm, gain_hbm))
    ]
    lines += [
        pltpu.make_async_copy(w.at[0], ref, sem.at[half + 3 + n])
        for n, (w, ref) in enumerate(zip(weights, kept))
    ]
    for copy in fetch + lines:
        copy.start()
    lists.wait()
    chosen = select_rows(halo_ref, rounds, rows)
    count = chosen.shape[0] // len(rounds)
    for b in range(half):
        fetch[b].wait()
        sent = dot(chosen, states[b][...]).astype(BF16)
        for n in range(len(rounds)):
            sends[b * len(rounds) + n][...] = sent[n * count : (n + 1) * count]
    for copy in lines:
        copy.wait()


def edge_matrices(rounds, index_ref, values_ref, near_ref, far_ref):
    tiles, listed, tile, _ = values_ref.shape
    entries = [[index_ref[r : r + 1, k : k + 1] for k in range(listed)] for r in range(tiles)]
    weights = [[values_ref[r, k].astype(F32) for k in range(listed)] for r in range(tiles)]
    places = [(near_ref, c, c) for c in range(tiles)]
    for n, (axis, turn) in enumerate(rounds):
        at = lax.axis_index(AXES[axis])
        upper = 1 - lax.rem(at + turn, 2)
        partner = at + 2 * upper - 1
        there = jnp.logical_and(partner >= 0, partner < lax.axis_size(AXES[axis]))
        places.append((far_ref, n, jnp.where(there, tiles + 2 * axis + upper, -1)))
    for ref, column, name in places:
        for r in range(tiles):
            total = None
            for k in range(listed):
                if (k < 2) == (ref is near_ref):
                    part = jnp.where(entries[r][k] == name, 1.0, 0.0) * weights[r][k]
                    total = part if total is None else total + part
            block = (pl.ds(r * tile, tile), pl.ds(column * tile, tile))
            ref[block] = total.astype(BF16)


def local_kernel(layer, rounds, half, *rest):
    first = layer == 0
    if first:
        index_ref, values_ref, rest = rest[0], rest[1], rest[2:]
    else:
        near_edges, rest = rest[0], rest[1:]
    states, rest = rest[:half], rest[half:]
    msg_a, in_a, out_a, vec_a, msg_b, in_b, out_b, vec_b = rest[:8]
    bases, rest = rest[8 : 8 + half], rest[8 + half :]
    nears, rest = rest[:half], rest[half:]
    fold_ref, last_ref, gain_ref = rest[:3]
    if first:
        near_edges, far_edges = rest[3:]
        edge_matrices(rounds, index_ref, values_ref, near_edges, far_edges)
    mine = lax.axis_index("section") == layer
    width = msg_a.shape[-1]
    vec = jnp.where(mine, vec_a[...], vec_b[...])
    bias = vec[:, :width]
    gain_ref[...] = vec[:, width:]

    def work(msg, into, out):
        whole = out().astype(F32)
        last_ref[...] = (whole - jnp.mean(whole, axis=-1, keepdims=True)).astype(BF16)
        fold_ref[...] = dot(msg(), into(width)).astype(BF16)
        for state, base in zip(states, bases):
            base[...] = dot(state[...], into(0)) + bias

    @pl.when(mine)
    def _():
        work(lambda: msg_a[...], lambda at: in_a[at : at + width], lambda: out_a[...])

    @pl.when(jnp.logical_not(mine))
    def _():
        work(lambda: msg_b[0], lambda at: in_b[0, at : at + width], lambda: out_b[0])

    for state, near in zip(states, nears):
        near[...] = dot(near_edges[...], state[...])


def finish_kernel(rounds, last_layer, final, earlier, edges_ref, halo_ref, state_ref, *rest):
    base_ref, near_ref, fold_ref, last_ref, gain_ref = rest[:5]
    recvs, rest = rest[5 : 5 + len(rounds)], rest[5 + len(rounds) :]
    before, rest = rest[:earlier], rest[earlier:]
    out_ref, rest = rest[0], rest[1:]
    sends, rest = ((), rest) if last_layer else (rest[: len(rounds)], rest[len(rounds) :])
    rows, width = base_ref.shape
    writes = []
    for n, ready in enumerate(before):
        writes.append(pltpu.make_async_copy(ready, out_ref.at[n], rest[1].at[n]))
        writes[n].start()
    came = jnp.concatenate([recv[...] for recv in recvs], axis=0)
    total = (dot(edges_ref[...], came) + near_ref[...]).astype(BF16)
    pre = base_ref[...] + dot(total, fold_ref[...])
    off = dot(jnp.maximum(pre, 0.0).astype(BF16), last_ref[...])
    cut = 2 * rows // 3 // 128 * 128
    for low, high in ((0, cut), (cut, rows)):
        some = off[low:high]
        var = jnp.mean(some * some, axis=-1, keepdims=True)
        normed = some * lax.rsqrt(var + 1e-05)
        at = pl.ds(low, high - low)
        fresh = (state_ref[at, :].astype(F32) + gain_ref[...] * normed).astype(BF16)
        if final:
            done, sem = rest
            done[at, :] = fresh
            writes.append(
                pltpu.make_async_copy(
                    done.at[at, :], out_ref.at[earlier, at, :], sem.at[len(writes)]
                )
            )
            writes[-1].start()
        else:
            out_ref[at, :] = fresh
    if sends:
        sent = dot(select_rows(halo_ref, rounds, rows), out_ref[...]).astype(BF16)
        count = sends[0].shape[0]
        for n, ref in enumerate(sends):
            ref[...] = sent[n * count : (n + 1) * count]
    for copy in writes:
        copy.wait()


VMEM = pl.BlockSpec(memory_space=pltpu.VMEM)
HBM = pl.BlockSpec(memory_space=pltpu.HBM)


def shards(nodes, tile_index, tile_values, halo_rows, w_msg, w_in, w_out, bias, gain):
    snaps, rows, width = nodes.shape
    sections = lax.axis_size("section")
    half = snaps // sections
    tiles, _, tile, _ = tile_values.shape
    rounds = meetings([lax.axis_size(name) for name in AXES])
    block = jax.ShapeDtypeStruct((tile, width), BF16)
    plane = jax.ShapeDtypeStruct((rows, width), BF16)
    wide = jax.ShapeDtypeStruct((rows, width), F32)
    square = jax.ShapeDtypeStruct((width, width), BF16)
    line = jax.ShapeDtypeStruct((1, width), F32)
    swaps = len(rounds)
    params = pltpu.CompilerParams(vmem_limit_bytes=LIMIT)
    in_hbm = lambda a: pltpu.with_memory_space_constraint(a, pltpu.HBM)

    def cost(matmul_rows):
        return pl.CostEstimate(
            flops=2 * matmul_rows * width * width,
            bytes_accessed=4 * matmul_rows * width,
            transcendentals=0,
        )

    mine = (w_msg, w_in, w_out)
    cross = [(0, 1), (1, 0)]
    other = tuple(lax.ppermute(w, "section", cross) for w in mine)
    picked = pl.pallas_call(
        functools.partial(pick_kernel, rounds, half),
        out_shape=[plane] * half
        + [jax.ShapeDtypeStruct((1, 2 * width), F32)]
        + [jax.ShapeDtypeStruct(w.shape[1:], BF16) for w in mine]
        + [block] * (half * swaps),
        in_specs=[HBM] * 7,
        out_specs=[VMEM] * (half + 4 + half * swaps),
        scratch_shapes=[
            pltpu.VMEM(halo_rows.shape, jnp.int32),
            pltpu.SemaphoreType.DMA((half + 6,)),
        ],
        cost_estimate=cost(half * rows),
        compiler_params=params,
        name="pick",
    )(*(in_hbm(a) for a in (halo_rows, nodes, bias, gain) + mine))
    states, vec, kept = picked[:half], picked[half], picked[half + 1 : half + 4]
    sends = [picked[half + 4 + b * swaps : half + 4 + (b + 1) * swaps] for b in range(half)]
    weights = (*kept, vec, *other, lax.ppermute(vec, "section", cross))

    def local(layer, edges, states):
        first = layer == 0
        matrices = [(rows, rows), (rows, swaps * tile)] if first else []
        results = pl.pallas_call(
            functools.partial(local_kernel, layer, rounds, half),
            out_shape=[wide] * (2 * half)
            + [square, square, line]
            + [jax.ShapeDtypeStruct(m, BF16) for m in matrices],
            in_specs=[VMEM] * (len(edges) + half + 8),
            out_specs=[VMEM] * (2 * half + 3 + len(matrices)),
            cost_estimate=cost(2 * half * rows + width),
            compiler_params=params,
            name=f"local{layer}",
        )(*edges, *states, *weights)
        return results[:half], results[half : 2 * half], results[2 * half :]

    for layer in range(2):
        final = layer == 1
        if final:
            bases, nears, shared = local(1, (near_edges,), states)
        else:
            bases, nears, shared = local(0, (tile_index, tile_values), states)
            near_edges, far_edges = shared[3:]
            bases, sends[1:] = lax.optimization_barrier((bases, sends[1:]))
        got = [[swap(sent, *turn) for sent, turn in zip(sends[b], rounds)] for b in range(half)]
        fresh, sends = [], []
        for b in range(half):
            ending = final and b == half - 1
            before = fresh if ending else []
            scratch = []
            if ending:
                scratch = [pltpu.VMEM((rows, width), BF16), pltpu.SemaphoreType.DMA((half + 1,))]
            results = pl.pallas_call(
                functools.partial(finish_kernel, rounds, final, ending, len(before)),
                out_shape=[jax.ShapeDtypeStruct((half, rows, width), BF16) if ending else plane]
                + ([] if final else [block] * swaps),
                in_specs=[VMEM] * (8 + swaps + len(before)),
                out_specs=[HBM if ending else VMEM] + ([] if final else [VMEM] * swaps),
                scratch_shapes=scratch,
                cost_estimate=cost((3 if final else 4) * rows),
                compiler_params=params,
                name=f"finish{layer}",
            )(
                far_edges, halo_rows, states[b], bases[b], nears[b], *shared[:3],
                *got[b], *before,
            )
            fresh.append(results[0])
            sends.append(results[1:])
        states = fresh
    return states[-1]


def solution(mesh):
    slab = ("groups", "slabx", "slaby")
    in_specs = (
        P(None, slab, None),
        P(slab, None),
        P(slab, None, None, None),
        P(slab, None, None),
        P("section", None, None),
        P("section", None, None),
        P("section", None, None),
        P("section", None),
        P("section", None),
    )
    out_specs = P("section", slab, None)
    return jax.shard_map(shards, mesh=mesh, in_specs=in_specs, out_specs=out_specs, check_vma=False)
```

```python
import functools

import jax
import jax.numpy as jnp
from jax import lax
from jax.experimental import pallas as pl
from jax.experimental.pallas import tpu as pltpu
from jax.sharding import PartitionSpec as P

F32 = jnp.float32
BF16 = jnp.bfloat16
LIMIT = 24 * 1024 * 1024
PICK = 30
AXES = ("slabx", "slaby")


def dot(a, b):
    return jnp.dot(a, b, preferred_element_type=F32)


def meetings(sizes):
    return [(axis, turn) for turn in range(2) for axis in (1, 0) if sizes[axis] > 1 + turn]


def swap(block, axis, turn):
    names = (AXES[axis], "section")
    size, cores = lax.axis_size(names[0]), lax.axis_size(names[1])
    route = []
    for at in range(size):
        partner = at + 1 if (at + turn) % 2 == 0 else at - 1
        for core in range(cores):
            there = (partner, core) if 0 <= partner < size else (at, cores - 1 - core)
            route.append((at * cores + core, there[0] * cores + there[1]))
    return lax.ppermute(block, names, route)


def select_rows(halo_ref, rounds, rows):
    picks = []
    for axis, turn in rounds:
        odd = lax.rem(lax.axis_index(AXES[axis]), 2)
        which = 2 * axis + (odd if turn == 0 else 1 - odd)
        listed = halo_ref[0, pl.ds(which, 1), :]
        count = listed.shape[1]
        down = jnp.transpose(jnp.broadcast_to(listed, (count, count)))
        for at in range(0, rows, count):
            columns = lax.broadcasted_iota(jnp.int32, (count, count), 1) + at
            picks.append((down == columns).astype(F32).astype(BF16))
    per = rows // count
    return jnp.concatenate(
        [
            jnp.concatenate(picks[n * per : (n + 1) * per], axis=1)
            for n in range(len(rounds))
        ],
        axis=0,
    )


def pick_kernel(rounds, half, halo_hbm, nodes_ref, bias_hbm, gain_hbm, *rest):
    states, rest = rest[:half], rest[half:]
    vec_ref, chosen_ref, rest = rest[0], rest[1], rest[2:]
    sends, (halo_ref, sem) = rest[: len(rounds)], rest[len(rounds) :]
    rows, width = states[0].shape
    section = lax.axis_index("section")
    lists = pltpu.make_async_copy(halo_hbm, halo_ref, sem.at[0])
    lists.start()
    fetch = [
        pltpu.make_async_copy(nodes_ref.at[section * half + b], states[b], sem.at[1 + b])
        for b in range(half)
    ]
    fetch += [
        pltpu.make_async_copy(line, vec_ref.at[:, pl.ds(n * width, width)], sem.at[half + 1 + n])
        for n, line in enumerate((bias_hbm, gain_hbm))
    ]
    for copy in fetch:
        copy.start()
    lists.wait()
    chosen = select_rows(halo_ref, rounds, rows)
    chosen_ref[...] = chosen
    fetch[0].wait()
    share(dot(chosen, states[0][...]), sends)
    for copy in fetch[1:]:
        copy.wait()


def share(sent, sends):
    count = sends[0].shape[0]
    for n, ref in enumerate(sends):
        ref[...] = sent[n * count : (n + 1) * count].astype(BF16)


def edge_matrices(rounds, index_ref, values_ref, near_ref, far_ref):
    tiles, listed, tile, _ = values_ref.shape
    entries = [[index_ref[r : r + 1, k : k + 1] for k in range(listed)] for r in range(tiles)]
    weights = [[values_ref[r, k].astype(F32) for k in range(listed)] for r in range(tiles)]
    places = [(near_ref, c, c) for c in range(tiles)]
    for n, (axis, turn) in enumerate(rounds):
        at = lax.axis_index(AXES[axis])
        upper = 1 - lax.rem(at + turn, 2)
        partner = at + 2 * upper - 1
        there = jnp.logical_and(partner >= 0, partner < lax.axis_size(AXES[axis]))
        places.append((far_ref, n, jnp.where(there, tiles + 2 * axis + upper, -1)))
    for ref, column, name in places:
        for r in range(tiles):
            total = None
            for k in range(listed):
                if (k < 2) == (ref is near_ref):
                    part = jnp.where(entries[r][k] == name, 1.0, 0.0) * weights[r][k]
                    total = part if total is None else total + part
            block = (pl.ds(r * tile, tile), pl.ds(column * tile, tile))
            ref[block] = total.astype(BF16)


def early_kernel(rounds, half, index_ref, values_ref, vec_ref, chosen_ref, *rest):
    states, rest = rest[:half], rest[half:]
    near_edges, far_edges, passed_ref, rest = rest[0], rest[1], rest[2], rest[3:]
    nears, sends = rest[:half], rest[half:]
    passed_ref[...] = vec_ref[...]
    for b in range(1, half):
        some = sends[(b - 1) * len(rounds) : b * len(rounds)]
        share(dot(chosen_ref[...], states[b][...]), some)
    edge_matrices(rounds, index_ref, values_ref, near_edges, far_edges)
    for state, near in zip(states, nears):
        near[...] = dot(near_edges[...], state[...])


def local_kernel(layer, half, *rest):
    if layer > 0:
        near_edges, rest = rest[0], rest[1:]
    states, rest = rest[:half], rest[half:]
    msg_a, in_a, out_a, vec_a, msg_b, in_b, out_b, vec_b = rest[:8]
    bases, rest = rest[8 : 8 + half], rest[8 + half :]
    fold_ref, last_ref, gain_ref, nears = rest[0], rest[1], rest[2], rest[3:]
    mine = lax.axis_index("section") == layer
    width = msg_a.shape[-1]
    vec = jnp.where(mine, vec_a[...], vec_b[...])
    bias = vec[:, :width]
    gain_ref[...] = vec[:, width:]

    def work(msg, into, out):
        whole = out[0].astype(F32)
        last_ref[...] = (whole - jnp.mean(whole, axis=-1, keepdims=True)).astype(BF16)
        fold_ref[...] = dot(msg[0], into[0, width:]).astype(BF16)
        for state, base in zip(states, bases):
            base[...] = dot(state[...], into[0, :width]) + bias

    @pl.when(mine)
    def _():
        work(msg_a, in_a, out_a)

    @pl.when(jnp.logical_not(mine))
    def _():
        work(msg_b, in_b, out_b)

    for state, near in zip(states, nears):
        near[...] = dot(near_edges[...], state[...])


def finish_kernel(rounds, last_layer, final, earlier, edges_ref, chosen_ref, state_ref, *rest):
    base_ref, near_ref, fold_ref, last_ref, gain_ref = rest[:5]
    recvs, rest = rest[5 : 5 + len(rounds)], rest[5 + len(rounds) :]
    before, rest = rest[:earlier], rest[earlier:]
    out_ref, rest = rest[0], rest[1:]
    sends, rest = ((), rest) if last_layer else (rest[: len(rounds)], rest[len(rounds) :])
    rows, width = base_ref.shape
    writes = []
    for n, ready in enumerate(before):
        writes.append(pltpu.make_async_copy(ready, out_ref.at[n], rest[1].at[n]))
        writes[n].start()
    came = jnp.concatenate([recv[...] for recv in recvs], axis=0)
    total = (dot(edges_ref[...], came) + near_ref[...]).astype(BF16)
    pre = base_ref[...] + dot(total, fold_ref[...])
    off = dot(jnp.maximum(pre, 0.0).astype(BF16), last_ref[...])
    cut = 2 * rows // 3 // 128 * 128
    for low, high in ((0, cut), (cut, rows)):
        some = off[low:high]
        var = jnp.mean(some * some, axis=-1, keepdims=True)
        normed = some * lax.rsqrt(var + 1e-05)
        at = pl.ds(low, high - low)
        fresh = (state_ref[at, :].astype(F32) + gain_ref[...] * normed).astype(BF16)
        if final:
            done, sem = rest
            done[at, :] = fresh
            writes.append(
                pltpu.make_async_copy(
                    done.at[at, :], out_ref.at[earlier, at, :], sem.at[len(writes)]
                )
            )
            writes[-1].start()
        else:
            out_ref[at, :] = fresh
    if sends:
        share(dot(chosen_ref[...], out_ref[...]), sends)
    for copy in writes:
        copy.wait()


VMEM = pl.BlockSpec(memory_space=pltpu.VMEM)
HBM = pl.BlockSpec(memory_space=pltpu.HBM)


def shards(nodes, tile_index, tile_values, halo_rows, w_msg, w_in, w_out, bias, gain):
    snaps, rows, width = nodes.shape
    sections = lax.axis_size("section")
    half = snaps // sections
    tiles, _, tile, _ = tile_values.shape
    rounds = meetings([lax.axis_size(name) for name in AXES])
    block = jax.ShapeDtypeStruct((tile, width), BF16)
    plane = jax.ShapeDtypeStruct((rows, width), BF16)
    wide = jax.ShapeDtypeStruct((rows, width), F32)
    square = jax.ShapeDtypeStruct((width, width), BF16)
    line = jax.ShapeDtypeStruct((1, width), F32)
    swaps = len(rounds)
    params = pltpu.CompilerParams(vmem_limit_bytes=LIMIT)
    in_hbm = lambda a: pltpu.with_memory_space_constraint(a, pltpu.HBM)

    def cost(matmul_rows):
        return pl.CostEstimate(
            flops=2 * matmul_rows * width * width,
            bytes_accessed=4 * matmul_rows * width,
            transcendentals=0,
        )

    mine = (w_msg, w_in, w_out)
    cross = [(0, 1), (1, 0)]
    other = tuple(lax.ppermute(w, "section", cross) for w in mine)
    matrix = lambda columns: jax.ShapeDtypeStruct((rows, columns), BF16)
    picks = jax.ShapeDtypeStruct((swaps * tile, rows), BF16)
    vec_shape = jax.ShapeDtypeStruct((1, 2 * width), F32)
    picked = pl.pallas_call(
        functools.partial(pick_kernel, rounds, half),
        out_shape=[plane] * half + [vec_shape, picks] + [block] * swaps,
        in_specs=[HBM] * 4,
        out_specs=[VMEM] * (half + 2 + swaps),
        scratch_shapes=[
            pltpu.VMEM(halo_rows.shape, jnp.int32),
            pltpu.SemaphoreType.DMA((half + 3,)),
        ],
        cost_estimate=cost(PICK * half * rows),
        compiler_params=params,
        name="pick",
    )(*(in_hbm(a) for a in (halo_rows, nodes, bias, gain)))
    states, (vec, chosen), sends = picked[:half], picked[half : half + 2], [picked[half + 2 :]]
    early = pl.pallas_call(
        functools.partial(early_kernel, rounds, half),
        out_shape=[matrix(rows), matrix(swaps * tile), vec_shape]
        + [wide] * half
        + [block] * (swaps * (half - 1)),
        in_specs=[VMEM] * (4 + half),
        out_specs=[VMEM] * (3 + half + swaps * (half - 1)),
        cost_estimate=cost(2 * half * rows),
        compiler_params=params,
        name="early",
    )(tile_index, tile_values, vec, chosen, *states)
    near_edges, far_edges, vec = early[:3]
    own_parts, late = early[3 : 3 + half], early[3 + half :]
    sends += [late[b * swaps : (b + 1) * swaps] for b in range(half - 1)]
    weights = (*mine, vec, *other, lax.ppermute(vec, "section", cross))

    def local(layer, edges, states):
        count = half if layer > 0 else 0
        results = pl.pallas_call(
            functools.partial(local_kernel, layer, half),
            out_shape=[wide] * half + [square, square, line] + [wide] * count,
            in_specs=[VMEM] * (len(edges) + half + 8),
            out_specs=[VMEM] * (half + 3 + count),
            cost_estimate=cost(2 * half * rows + width),
            compiler_params=params,
            name=f"local{layer}",
        )(*edges, *states, *weights)
        return results[:half], results[half : half + 3], results[half + 3 :]

    for layer in range(2):
        final = layer == 1
        bases, shared, nears = local(layer, (near_edges,) if final else (), states)
        nears = nears if final else own_parts
        got = [[swap(sent, *turn) for sent, turn in zip(sends[b], rounds)] for b in range(half)]
        fresh, sends = [], []
        for b in range(half):
            ending = final and b == half - 1
            before = fresh if ending else []
            scratch = []
            if ending:
                scratch = [pltpu.VMEM((rows, width), BF16), pltpu.SemaphoreType.DMA((half + 1,))]
            results = pl.pallas_call(
                functools.partial(finish_kernel, rounds, final, ending, len(before)),
                out_shape=[jax.ShapeDtypeStruct((half, rows, width), BF16) if ending else plane]
                + ([] if final else [block] * swaps),
                in_specs=[VMEM] * (8 + swaps + len(before)),
                out_specs=[HBM if ending else VMEM] + ([] if final else [VMEM] * swaps),
                scratch_shapes=scratch,
                cost_estimate=cost((3 if final else 4) * rows),
                compiler_params=params,
                name=f"finish{layer}",
            )(
                far_edges, chosen, states[b], bases[b], nears[b], *shared,
                *got[b], *before,
            )
            fresh.append(results[0])
            sends.append(results[1:])
        states = fresh
    return states[-1]


def solution(mesh):
    slab = ("groups", "slabx", "slaby")
    in_specs = (
        P(None, slab, None),
        P(slab, None),
        P(slab, None, None, None),
        P(slab, None, None),
        P("section", None, None),
        P("section", None, None),
        P("section", None, None),
        P("section", None),
        P("section", None),
    )
    out_specs = P("section", slab, None)
    return jax.shard_map(shards, mesh=mesh, in_specs=in_specs, out_specs=out_specs, check_vma=False)
```

```python
import functools

import jax
import jax.numpy as jnp
from jax import lax
from jax.experimental import pallas as pl
from jax.experimental.pallas import tpu as pltpu
from jax.sharding import PartitionSpec as P

F32 = jnp.float32
BF16 = jnp.bfloat16
LIMIT = 24 * 1024 * 1024
PICK = 30
ORDERS = [[[2, 1, 0], [0, 1, 2]], [[1, 0, 2], [0, 1, 2]]]
AXES = ("slabx", "slaby")


def dot(a, b):
    return jnp.dot(a, b, preferred_element_type=F32)


def meetings(sizes):
    return [(axis, turn) for turn in range(2) for axis in (1, 0) if sizes[axis] > 1 + turn]


def swap(block, axis, turn):
    names = (AXES[axis], "section")
    size, cores = lax.axis_size(names[0]), lax.axis_size(names[1])
    route = []
    for at in range(size):
        partner = at + 1 if (at + turn) % 2 == 0 else at - 1
        for core in range(cores):
            there = (partner, core) if 0 <= partner < size else (at, cores - 1 - core)
            route.append((at * cores + core, there[0] * cores + there[1]))
    return lax.ppermute(block, names, route)


def turns_of(layer, snap, rounds):
    return ORDERS[layer][min(snap, 1)] if len(rounds) == 3 else list(range(len(rounds)))


def select_rows(halo_ref, rounds, rows):
    picks = []
    for axis, turn in rounds:
        odd = lax.rem(lax.axis_index(AXES[axis]), 2)
        which = 2 * axis + (odd if turn == 0 else 1 - odd)
        listed = halo_ref[0, pl.ds(which, 1), :]
        count = listed.shape[1]
        down = jnp.transpose(jnp.broadcast_to(listed, (count, count)))
        for at in range(0, rows, count):
            columns = lax.broadcasted_iota(jnp.int32, (count, count), 1) + at
            picks.append((down == columns).astype(F32).astype(BF16))
    per = rows // count
    return jnp.concatenate(
        [
            jnp.concatenate(picks[n * per : (n + 1) * per], axis=1)
            for n in range(len(rounds))
        ],
        axis=0,
    )


def pick_kernel(rounds, half, halo_hbm, nodes_ref, bias_hbm, gain_hbm, *rest):
    states, rest = rest[:half], rest[half:]
    vec_ref, chosen_ref, rest = rest[0], rest[1], rest[2:]
    sends, (halo_ref, sem) = rest[: len(rounds)], rest[len(rounds) :]
    rows, width = states[0].shape
    section = lax.axis_index("section")
    lists = pltpu.make_async_copy(halo_hbm, halo_ref, sem.at[0])
    lists.start()
    fetch = [
        pltpu.make_async_copy(nodes_ref.at[section * half + b], states[b], sem.at[1 + b])
        for b in range(half)
    ]
    fetch += [
        pltpu.make_async_copy(line, vec_ref.at[:, pl.ds(n * width, width)], sem.at[half + 1 + n])
        for n, line in enumerate((bias_hbm, gain_hbm))
    ]
    for copy in fetch:
        copy.start()
    lists.wait()
    chosen = select_rows(halo_ref, rounds, rows)
    chosen_ref[...] = chosen
    fetch[0].wait()
    share(dot(chosen, states[0][...]), sends, turns_of(0, 0, rounds))
    for copy in fetch[1:]:
        copy.wait()


def share(sent, sends, order):
    count = sends[0].shape[0]
    for ref, n in zip(sends, order):
        ref[...] = sent[n * count : (n + 1) * count].astype(BF16)


def edge_matrices(rounds, index_ref, values_ref, near_ref, far_ref):
    tiles, listed, tile, _ = values_ref.shape
    entries = [[index_ref[r : r + 1, k : k + 1] for k in range(listed)] for r in range(tiles)]
    weights = [[values_ref[r, k].astype(F32) for k in range(listed)] for r in range(tiles)]
    places = [(near_ref, c, c) for c in range(tiles)]
    for n, (axis, turn) in enumerate(rounds):
        at = lax.axis_index(AXES[axis])
        upper = 1 - lax.rem(at + turn, 2)
        partner = at + 2 * upper - 1
        there = jnp.logical_and(partner >= 0, partner < lax.axis_size(AXES[axis]))
        places.append((far_ref, n, jnp.where(there, tiles + 2 * axis + upper, -1)))
    for ref, column, name in places:
        for r in range(tiles):
            total = None
            for k in range(listed):
                if (k < 2) == (ref is near_ref):
                    part = jnp.where(entries[r][k] == name, 1.0, 0.0) * weights[r][k]
                    total = part if total is None else total + part
            block = (pl.ds(r * tile, tile), pl.ds(column * tile, tile))
            ref[block] = total.astype(BF16)


def early_kernel(rounds, half, index_ref, values_ref, vec_ref, chosen_ref, *rest):
    states, rest = rest[:half], rest[half:]
    near_edges, far_edges, passed_ref, rest = rest[0], rest[1], rest[2], rest[3:]
    nears, sends = rest[:half], rest[half:]
    passed_ref[...] = vec_ref[...]
    for b in range(1, half):
        some = sends[(b - 1) * len(rounds) : b * len(rounds)]
        share(dot(chosen_ref[...], states[b][...]), some, turns_of(0, b, rounds))
    edge_matrices(rounds, index_ref, values_ref, near_edges, far_edges)
    for state, near in zip(states, nears):
        near[...] = dot(near_edges[...], state[...])


def local_kernel(layer, half, *rest):
    if layer > 0:
        near_edges, rest = rest[0], rest[1:]
    states, rest = rest[:half], rest[half:]
    msg_a, in_a, out_a, vec_a, msg_b, in_b, out_b, vec_b = rest[:8]
    bases, rest = rest[8 : 8 + half], rest[8 + half :]
    fold_ref, last_ref, gain_ref, nears = rest[0], rest[1], rest[2], rest[3:]
    mine = lax.axis_index("section") == layer
    width = msg_a.shape[-1]
    vec = jnp.where(mine, vec_a[...], vec_b[...])
    bias = vec[:, :width]
    gain_ref[...] = vec[:, width:]

    def work(msg, into, out):
        whole = out[0].astype(F32)
        last_ref[...] = (whole - jnp.mean(whole, axis=-1, keepdims=True)).astype(BF16)
        fold_ref[...] = dot(msg[0], into[0, width:]).astype(BF16)
        for state, base in zip(states, bases):
            base[...] = dot(state[...], into[0, :width]) + bias

    @pl.when(mine)
    def _():
        work(msg_a, in_a, out_a)

    @pl.when(jnp.logical_not(mine))
    def _():
        work(msg_b, in_b, out_b)

    for state, near in zip(states, nears):
        near[...] = dot(near_edges[...], state[...])


def finish_kernel(snap, rounds, last_layer, final, earlier, edges_ref, chosen_ref, state_ref, *rest):
    base_ref, near_ref, fold_ref, last_ref, gain_ref = rest[:5]
    recvs, rest = rest[5 : 5 + len(rounds)], rest[5 + len(rounds) :]
    before, rest = rest[:earlier], rest[earlier:]
    out_ref, rest = rest[0], rest[1:]
    sends, rest = ((), rest) if last_layer else (rest[: len(rounds)], rest[len(rounds) :])
    rows, width = base_ref.shape
    writes = []
    for n, ready in enumerate(before):
        writes.append(pltpu.make_async_copy(ready, out_ref.at[n], rest[1].at[n]))
        writes[n].start()
    order = turns_of(int(last_layer), snap, rounds)
    came = [recvs[order.index(n)][...] for n in range(len(rounds))]
    came = jnp.concatenate(came, axis=0)
    total = (dot(edges_ref[...], came) + near_ref[...]).astype(BF16)
    pre = base_ref[...] + dot(total, fold_ref[...])
    off = dot(jnp.maximum(pre, 0.0).astype(BF16), last_ref[...])
    cut = 2 * rows // 3 // 128 * 128
    for low, high in ((0, cut), (cut, rows)):
        some = off[low:high]
        var = jnp.mean(some * some, axis=-1, keepdims=True)
        normed = some * lax.rsqrt(var + 1e-05)
        at = pl.ds(low, high - low)
        fresh = (state_ref[at, :].astype(F32) + gain_ref[...] * normed).astype(BF16)
        if final:
            done, sem = rest
            done[at, :] = fresh
            writes.append(
                pltpu.make_async_copy(
                    done.at[at, :], out_ref.at[earlier, at, :], sem.at[len(writes)]
                )
            )
            writes[-1].start()
        else:
            out_ref[at, :] = fresh
    if sends:
        share(dot(chosen_ref[...], out_ref[...]), sends, turns_of(1, snap, rounds))
    for copy in writes:
        copy.wait()


VMEM = pl.BlockSpec(memory_space=pltpu.VMEM)
HBM = pl.BlockSpec(memory_space=pltpu.HBM)


def shards(nodes, tile_index, tile_values, halo_rows, w_msg, w_in, w_out, bias, gain):
    snaps, rows, width = nodes.shape
    sections = lax.axis_size("section")
    half = snaps // sections
    tiles, _, tile, _ = tile_values.shape
    rounds = meetings([lax.axis_size(name) for name in AXES])
    block = jax.ShapeDtypeStruct((tile, width), BF16)
    plane = jax.ShapeDtypeStruct((rows, width), BF16)
    wide = jax.ShapeDtypeStruct((rows, width), F32)
    square = jax.ShapeDtypeStruct((width, width), BF16)
    line = jax.ShapeDtypeStruct((1, width), F32)
    swaps = len(rounds)
    params = pltpu.CompilerParams(vmem_limit_bytes=LIMIT)
    in_hbm = lambda a: pltpu.with_memory_space_constraint(a, pltpu.HBM)

    def cost(matmul_rows):
        return pl.CostEstimate(
            flops=2 * matmul_rows * width * width,
            bytes_accessed=4 * matmul_rows * width,
            transcendentals=0,
        )

    mine = (w_msg, w_in, w_out)
    cross = [(0, 1), (1, 0)]
    other = tuple(lax.ppermute(w, "section", cross) for w in mine)
    matrix = lambda columns: jax.ShapeDtypeStruct((rows, columns), BF16)
    picks = jax.ShapeDtypeStruct((swaps * tile, rows), BF16)
    vec_shape = jax.ShapeDtypeStruct((1, 2 * width), F32)
    picked = pl.pallas_call(
        functools.partial(pick_kernel, rounds, half),
        out_shape=[plane] * half + [vec_shape, picks] + [block] * swaps,
        in_specs=[HBM] * 4,
        out_specs=[VMEM] * (half + 2 + swaps),
        scratch_shapes=[
            pltpu.VMEM(halo_rows.shape, jnp.int32),
            pltpu.SemaphoreType.DMA((half + 3,)),
        ],
        cost_estimate=cost(PICK * half * rows),
        compiler_params=params,
        name="pick",
    )(*(in_hbm(a) for a in (halo_rows, nodes, bias, gain)))
    states, (vec, chosen), sends = picked[:half], picked[half : half + 2], [picked[half + 2 :]]
    early = pl.pallas_call(
        functools.partial(early_kernel, rounds, half),
        out_shape=[matrix(rows), matrix(swaps * tile), vec_shape]
        + [wide] * half
        + [block] * (swaps * (half - 1)),
        in_specs=[VMEM] * (4 + half),
        out_specs=[VMEM] * (3 + half + swaps * (half - 1)),
        cost_estimate=cost(2 * half * rows),
        compiler_params=params,
        name="early",
    )(tile_index, tile_values, vec, chosen, *states)
    near_edges, far_edges, vec = early[:3]
    own_parts, late = early[3 : 3 + half], early[3 + half :]
    sends += [late[b * swaps : (b + 1) * swaps] for b in range(half - 1)]
    weights = (*mine, vec, *other, lax.ppermute(vec, "section", cross))

    def local(layer, edges, states):
        count = half if layer > 0 else 0
        results = pl.pallas_call(
            functools.partial(local_kernel, layer, half),
            out_shape=[wide] * half + [square, square, line] + [wide] * count,
            in_specs=[VMEM] * (len(edges) + half + 8),
            out_specs=[VMEM] * (half + 3 + count),
            cost_estimate=cost(2 * half * rows + width),
            compiler_params=params,
            name=f"local{layer}",
        )(*edges, *states, *weights)
        return results[:half], results[half : half + 3], results[half + 3 :]

    for layer in range(2):
        final = layer == 1
        bases, shared, nears = local(layer, (near_edges,) if final else (), states)
        nears = nears if final else own_parts
        got = []
        for b in range(half):
            order = turns_of(layer, b, rounds)
            got.append([swap(sent, *rounds[n]) for sent, n in zip(sends[b], order)])
        fresh, sends = [], []
        for b in range(half):
            ending = final and b == half - 1
            before = fresh if ending else []
            scratch = []
            if ending:
                scratch = [pltpu.VMEM((rows, width), BF16), pltpu.SemaphoreType.DMA((half + 1,))]
            results = pl.pallas_call(
                functools.partial(finish_kernel, b, rounds, final, ending, len(before)),
                out_shape=[jax.ShapeDtypeStruct((half, rows, width), BF16) if ending else plane]
                + ([] if final else [block] * swaps),
                in_specs=[VMEM] * (8 + swaps + len(before)),
                out_specs=[HBM if ending else VMEM] + ([] if final else [VMEM] * swaps),
                scratch_shapes=scratch,
                cost_estimate=cost((3 if final else 4) * rows),
                compiler_params=params,
                name=f"finish{layer}",
            )(
                far_edges, chosen, states[b], bases[b], nears[b], *shared,
                *got[b], *before,
            )
            fresh.append(results[0])
            sends.append(results[1:])
        states = fresh
    return states[-1]


def solution(mesh):
    slab = ("groups", "slabx", "slaby")
    in_specs = (
        P(None, slab, None),
        P(slab, None),
        P(slab, None, None, None),
        P(slab, None, None),
        P("section", None, None),
        P("section", None, None),
        P("section", None, None),
        P("section", None),
        P("section", None),
    )
    out_specs = P("section", slab, None)
    return jax.shard_map(shards, mesh=mesh, in_specs=in_specs, out_specs=out_specs, check_vma=False)
```

```python
import functools

import jax
import jax.numpy as jnp
from jax import lax
from jax.experimental import pallas as pl
from jax.experimental.pallas import tpu as pltpu
from jax.sharding import PartitionSpec as P

F32 = jnp.float32
BF16 = jnp.bfloat16
LIMIT = 24 * 1024 * 1024
PICK = 30
ORDERS = [[[2, 1, 0], [1, 0, 2]], [[0, 1, 2], [0, 1, 2]]]
AXES = ("slabx", "slaby")


def dot(a, b):
    return jnp.dot(a, b, preferred_element_type=F32)


def meetings(sizes):
    return [(axis, turn) for turn in range(2) for axis in (1, 0) if sizes[axis] > 1 + turn]


def swap(block, axis, turn):
    names = (AXES[axis], "section")
    size, cores = lax.axis_size(names[0]), lax.axis_size(names[1])
    route = []
    for at in range(size):
        partner = at + 1 if (at + turn) % 2 == 0 else at - 1
        for core in range(cores):
            there = (partner, core) if 0 <= partner < size else (at, cores - 1 - core)
            route.append((at * cores + core, there[0] * cores + there[1]))
    return lax.ppermute(block, names, route)


def turns_of(layer, snap, rounds):
    return ORDERS[layer][min(snap, 1)] if len(rounds) == 3 else list(range(len(rounds)))


def select_rows(halo_ref, rounds, rows):
    picks = []
    for axis, turn in rounds:
        odd = lax.rem(lax.axis_index(AXES[axis]), 2)
        which = 2 * axis + (odd if turn == 0 else 1 - odd)
        listed = halo_ref[0, pl.ds(which, 1), :]
        count = listed.shape[1]
        down = jnp.transpose(jnp.broadcast_to(listed, (count, count)))
        for at in range(0, rows, count):
            columns = lax.broadcasted_iota(jnp.int32, (count, count), 1) + at
            picks.append((down == columns).astype(F32).astype(BF16))
    per = rows // count
    return jnp.concatenate(
        [
            jnp.concatenate(picks[n * per : (n + 1) * per], axis=1)
            for n in range(len(rounds))
        ],
        axis=0,
    )


def pick_kernel(rounds, half, halo_hbm, nodes_ref, bias_hbm, gain_hbm, *rest):
    states, rest = rest[:half], rest[half:]
    vec_ref, chosen_ref, rest = rest[0], rest[1], rest[2:]
    sends, (halo_ref, sem) = rest[: len(rounds)], rest[len(rounds) :]
    rows, width = states[0].shape
    section = lax.axis_index("section")
    lists = pltpu.make_async_copy(halo_hbm, halo_ref, sem.at[0])
    lists.start()
    fetch = [
        pltpu.make_async_copy(nodes_ref.at[section * half + b], states[b], sem.at[1 + b])
        for b in range(half)
    ]
    fetch += [
        pltpu.make_async_copy(line, vec_ref.at[:, pl.ds(n * width, width)], sem.at[half + 1 + n])
        for n, line in enumerate((bias_hbm, gain_hbm))
    ]
    for copy in fetch:
        copy.start()
    lists.wait()
    chosen = select_rows(halo_ref, rounds, rows)
    chosen_ref[...] = chosen
    fetch[0].wait()
    share(dot(chosen, states[0][...]), sends, turns_of(0, 0, rounds))
    for copy in fetch[1:]:
        copy.wait()


def share(sent, sends, order):
    count = sends[0].shape[0]
    for ref, n in zip(sends, order):
        ref[...] = sent[n * count : (n + 1) * count].astype(BF16)


def edge_matrices(rounds, index_ref, values_ref, near_ref, far_ref):
    tiles, listed, tile, _ = values_ref.shape
    entries = [[index_ref[r : r + 1, k : k + 1] for k in range(listed)] for r in range(tiles)]
    weights = [[values_ref[r, k].astype(F32) for k in range(listed)] for r in range(tiles)]
    places = [(near_ref, c, c) for c in range(tiles)]
    for n, (axis, turn) in enumerate(rounds):
        at = lax.axis_index(AXES[axis])
        upper = 1 - lax.rem(at + turn, 2)
        partner = at + 2 * upper - 1
        there = jnp.logical_and(partner >= 0, partner < lax.axis_size(AXES[axis]))
        places.append((far_ref, n, jnp.where(there, tiles + 2 * axis + upper, -1)))
    for ref, column, name in places:
        for r in range(tiles):
            total = None
            for k in range(listed):
                if (k < 2) == (ref is near_ref):
                    part = jnp.where(entries[r][k] == name, 1.0, 0.0) * weights[r][k]
                    total = part if total is None else total + part
            block = (pl.ds(r * tile, tile), pl.ds(column * tile, tile))
            ref[block] = total.astype(BF16)


def early_kernel(rounds, half, index_ref, values_ref, vec_ref, chosen_ref, *rest):
    states, rest = rest[:half], rest[half:]
    near_edges, far_edges, passed_ref, rest = rest[0], rest[1], rest[2], rest[3:]
    nears, sends = rest[:half], rest[half:]
    passed_ref[...] = vec_ref[...]
    for b in range(1, half):
        some = sends[(b - 1) * len(rounds) : b * len(rounds)]
        share(dot(chosen_ref[...], states[b][...]), some, turns_of(0, b, rounds))
    edge_matrices(rounds, index_ref, values_ref, near_edges, far_edges)
    for state, near in zip(states, nears):
        near[...] = dot(near_edges[...], state[...])


def local_kernel(layer, half, *rest):
    if layer > 0:
        near_edges, rest = rest[0], rest[1:]
    states, rest = rest[:half], rest[half:]
    msg_a, in_a, out_a, vec_a, msg_b, in_b, out_b, vec_b = rest[:8]
    bases, rest = rest[8 : 8 + half], rest[8 + half :]
    fold_ref, last_ref, gain_ref, nears = rest[0], rest[1], rest[2], rest[3:]
    mine = lax.axis_index("section") == layer
    width = msg_a.shape[-1]
    vec = jnp.where(mine, vec_a[...], vec_b[...])
    bias = vec[:, :width]
    gain_ref[...] = vec[:, width:]

    def work(msg, into, out):
        whole = out[0].astype(F32)
        last_ref[...] = (whole - jnp.mean(whole, axis=-1, keepdims=True)).astype(BF16)
        fold_ref[...] = dot(msg[0], into[0, width:]).astype(BF16)
        for state, base in zip(states, bases):
            base[...] = dot(state[...], into[0, :width]) + bias

    @pl.when(mine)
    def _():
        work(msg_a, in_a, out_a)

    @pl.when(jnp.logical_not(mine))
    def _():
        work(msg_b, in_b, out_b)

    for state, near in zip(states, nears):
        near[...] = dot(near_edges[...], state[...])


def finish_kernel(snap, rounds, last_layer, final, earlier, edges_ref, chosen_ref, state_ref, *rest):
    base_ref, near_ref, fold_ref, last_ref, gain_ref = rest[:5]
    recvs, rest = rest[5 : 5 + len(rounds)], rest[5 + len(rounds) :]
    before, rest = rest[:earlier], rest[earlier:]
    out_ref, rest = rest[0], rest[1:]
    sends, rest = ((), rest) if last_layer else (rest[: len(rounds)], rest[len(rounds) :])
    rows, width = base_ref.shape
    writes = []
    for n, ready in enumerate(before):
        writes.append(pltpu.make_async_copy(ready, out_ref.at[n], rest[1].at[n]))
        writes[n].start()
    order = turns_of(int(last_layer), snap, rounds)
    came = [recvs[order.index(n)][...] for n in range(len(rounds))]
    came = jnp.concatenate(came, axis=0)
    total = (dot(edges_ref[...], came) + near_ref[...]).astype(BF16)
    pre = base_ref[...] + dot(total, fold_ref[...])
    off = dot(jnp.maximum(pre, 0.0).astype(BF16), last_ref[...])
    cut = 2 * rows // 3 // 128 * 128
    for low, high in ((0, cut), (cut, rows)):
        some = off[low:high]
        var = jnp.mean(some * some, axis=-1, keepdims=True)
        normed = some * lax.rsqrt(var + 1e-05)
        at = pl.ds(low, high - low)
        fresh = (state_ref[at, :].astype(F32) + gain_ref[...] * normed).astype(BF16)
        if final:
            done, sem = rest
            done[at, :] = fresh
            writes.append(
                pltpu.make_async_copy(
                    done.at[at, :], out_ref.at[earlier, at, :], sem.at[len(writes)]
                )
            )
            writes[-1].start()
        else:
            out_ref[at, :] = fresh
    if sends:
        share(dot(chosen_ref[...], out_ref[...]), sends, turns_of(1, snap, rounds))
    for copy in writes:
        copy.wait()


VMEM = pl.BlockSpec(memory_space=pltpu.VMEM)
HBM = pl.BlockSpec(memory_space=pltpu.HBM)


def shards(nodes, tile_index, tile_values, halo_rows, w_msg, w_in, w_out, bias, gain):
    snaps, rows, width = nodes.shape
    sections = lax.axis_size("section")
    half = snaps // sections
    tiles, _, tile, _ = tile_values.shape
    rounds = meetings([lax.axis_size(name) for name in AXES])
    block = jax.ShapeDtypeStruct((tile, width), BF16)
    plane = jax.ShapeDtypeStruct((rows, width), BF16)
    wide = jax.ShapeDtypeStruct((rows, width), F32)
    square = jax.ShapeDtypeStruct((width, width), BF16)
    line = jax.ShapeDtypeStruct((1, width), F32)
    swaps = len(rounds)
    params = pltpu.CompilerParams(vmem_limit_bytes=LIMIT)
    in_hbm = lambda a: pltpu.with_memory_space_constraint(a, pltpu.HBM)

    def cost(matmul_rows):
        return pl.CostEstimate(
            flops=2 * matmul_rows * width * width,
            bytes_accessed=4 * matmul_rows * width,
            transcendentals=0,
        )

    mine = (w_msg, w_in, w_out)
    cross = [(0, 1), (1, 0)]
    other = tuple(lax.ppermute(w, "section", cross) for w in mine)
    matrix = lambda columns: jax.ShapeDtypeStruct((rows, columns), BF16)
    picks = jax.ShapeDtypeStruct((swaps * tile, rows), BF16)
    vec_shape = jax.ShapeDtypeStruct((1, 2 * width), F32)
    picked = pl.pallas_call(
        functools.partial(pick_kernel, rounds, half),
        out_shape=[plane] * half + [vec_shape, picks] + [block] * swaps,
        in_specs=[HBM] * 4,
        out_specs=[VMEM] * (half + 2 + swaps),
        scratch_shapes=[
            pltpu.VMEM(halo_rows.shape, jnp.int32),
            pltpu.SemaphoreType.DMA((half + 3,)),
        ],
        cost_estimate=cost(PICK * half * rows),
        compiler_params=params,
        name="pick",
    )(*(in_hbm(a) for a in (halo_rows, nodes, bias, gain)))
    states, (vec, chosen), sends = picked[:half], picked[half : half + 2], [picked[half + 2 :]]
    early = pl.pallas_call(
        functools.partial(early_kernel, rounds, half),
        out_shape=[matrix(rows), matrix(swaps * tile), vec_shape]
        + [wide] * half
        + [block] * (swaps * (half - 1)),
        in_specs=[VMEM] * (4 + half),
        out_specs=[VMEM] * (3 + half + swaps * (half - 1)),
        cost_estimate=cost(2 * half * rows),
        compiler_params=params,
        name="early",
    )(tile_index, tile_values, vec, chosen, *states)
    near_edges, far_edges, vec = early[:3]
    own_parts, late = early[3 : 3 + half], early[3 + half :]
    sends += [late[b * swaps : (b + 1) * swaps] for b in range(half - 1)]
    weights = (*mine, vec, *other, lax.ppermute(vec, "section", cross))

    def local(layer, edges, states):
        count = half if layer > 0 else 0
        results = pl.pallas_call(
            functools.partial(local_kernel, layer, half),
            out_shape=[wide] * half + [square, square, line] + [wide] * count,
            in_specs=[VMEM] * (len(edges) + half + 8),
            out_specs=[VMEM] * (half + 3 + count),
            cost_estimate=cost(2 * half * rows + width),
            compiler_params=params,
            name=f"local{layer}",
        )(*edges, *states, *weights)
        return results[:half], results[half : half + 3], results[half + 3 :]

    for layer in range(2):
        final = layer == 1
        bases, shared, nears = local(layer, (near_edges,) if final else (), states)
        nears = nears if final else own_parts
        got = []
        for b in range(half):
            order = turns_of(layer, b, rounds)
            got.append([swap(sent, *rounds[n]) for sent, n in zip(sends[b], order)])
        fresh, sends = [], []
        for b in range(half):
            ending = final and b == half - 1
            before = fresh if ending else []
            scratch = []
            if ending:
                scratch = [pltpu.VMEM((rows, width), BF16), pltpu.SemaphoreType.DMA((half + 1,))]
            results = pl.pallas_call(
                functools.partial(finish_kernel, b, rounds, final, ending, len(before)),
                out_shape=[jax.ShapeDtypeStruct((half, rows, width), BF16) if ending else plane]
                + ([] if final else [block] * swaps),
                in_specs=[VMEM] * (8 + swaps + len(before)),
                out_specs=[HBM if ending else VMEM] + ([] if final else [VMEM] * swaps),
                scratch_shapes=scratch,
                cost_estimate=cost((3 if final else 4) * rows),
                compiler_params=params,
                name=f"finish{layer}",
            )(
                far_edges, chosen, states[b], bases[b], nears[b], *shared,
                *got[b], *before,
            )
            fresh.append(results[0])
            sends.append(results[1:])
        states = fresh
    return states[-1]


def solution(mesh):
    slab = ("groups", "slabx", "slaby")
    in_specs = (
        P(None, slab, None),
        P(slab, None),
        P(slab, None, None, None),
        P(slab, None, None),
        P("section", None, None),
        P("section", None, None),
        P("section", None, None),
        P("section", None),
        P("section", None),
    )
    out_specs = P("section", slab, None)
    return jax.shard_map(shards, mesh=mesh, in_specs=in_specs, out_specs=out_specs, check_vma=False)
```
